512 devices in a mesh: ctx: 64 (over y, z), exp: 8 (over x, core).
Axes of the slice: x: 4, y: 4, z: 16, core: 2. Of those that a mesh axis runs over, the one named last changes fastest.
Arguments:
- queries: bfloat16 [8192, 4096], P('ctx', 'exp'), may hold values from -24 to 24
- key_rows: bfloat16 [8192, 1024], P('ctx', 'exp'), may hold values from -24 to 24
- mixer_input: bfloat16 [8192, 8192], P('ctx', 'exp'), may hold values from -32 to 32
- gate_input: bfloat16 [8192, 8192], P('ctx', 'exp'), may hold values from -6 to 6
- write_proj: bfloat16 [8192, 128], P('ctx'), may hold values from -0.5 to 0.5
- read_proj: bfloat16 [8192, 128], P('ctx'), may hold values from -0.5 to 0.5
- step_size: float32 [8192, 128], P('ctx', 'exp'), may hold values from 0.5 to 2
- log_decay: float32 [8192, 128], P('ctx', 'exp'), may hold values from -1.7 to 0
- skip_gain: float32 [128], P('exp'), may hold values from 0.5 to 2
- norm_gain: float32 [8192], P('exp'), may hold values from 0.1 to 1.9
- value_weight: bfloat16 [8192, 1024], P('exp'), may hold values from -0.09375 to 0.09375
Outputs:
- attention_out: bfloat16 [8192, 4096], P('ctx', 'exp')
- mixer_out: bfloat16 [8192, 8192], P('ctx', 'exp')
The draws below stay inside these ranges and needn't reach their ends.
All inputs are finite; a program needn't handle non-finite values.
Results may differ from the reference program's by a relative error of at most 0.018.
Values may be sent and summed in bfloat16 or wider, within the bound.
A program may use at most 64 MiB of HBM per device.

```python
import math
import jax
import jax.numpy as jnp
from jax import lax

QUERY_HEADS = 32
KEY_HEADS = 8
HEAD_DIM = 128
MIXER_HEADS = 128
MIXER_CHANNELS = 64
STATE_SIZE = 128
BLOCK_LEN = 128
SHARD_TOKENS = 128
PROMPT_TOKENS = 8192


def query_key_pair(base_key):
    key_query, key_keys = jax.random.split(base_key, 2)
    query_vals = jnp.clip(jax.random.normal(key_query, (PROMPT_TOKENS, QUERY_HEADS, HEAD_DIM), jnp.float32), -6.0, 6.0)
    key_vals = jnp.clip(jax.random.normal(key_keys, (PROMPT_TOKENS, KEY_HEADS, HEAD_DIM), jnp.float32), -6.0, 6.0)
    return (query_vals.reshape(PROMPT_TOKENS, QUERY_HEADS * HEAD_DIM), key_vals.reshape(PROMPT_TOKENS, KEY_HEADS * HEAD_DIM))


def draw_queries(key, part):
    return query_key_pair(jax.random.fold_in(key, 11))[0].astype(jnp.bfloat16)


def draw_key_rows(key, part):
    return query_key_pair(jax.random.fold_in(key, 11))[1].astype(jnp.bfloat16)


def draw_mixer_input(key, part):
    key_value, key_row = jax.random.split(jax.random.fold_in(key, 23))
    head_place = jnp.arange(MIXER_HEADS, dtype=jnp.float32) / max(MIXER_HEADS - 1, 1)
    values_raw = jnp.clip(jax.random.normal(key_value, (PROMPT_TOKENS, MIXER_HEADS * MIXER_CHANNELS), jnp.float32), -6.0, 6.0)
    row_scale = jnp.exp(jax.random.uniform(key_row, (PROMPT_TOKENS,), jnp.float32, math.log(0.3), math.log(3.0)))
    head_scale = 3.0 ** (0.5 * head_place)
    column_scale = jnp.repeat(head_scale, MIXER_CHANNELS)
    return (values_raw * row_scale[:, None] * column_scale[None, :]).astype(jnp.bfloat16)


def draw_log_decay(key, part):
    key_slow, key_fast, key_rate, key_rough, key_shard, key_location, key_penalty = jax.random.split(jax.random.fold_in(key, 37), 7)
    slow_share = 0.5
    slow_heads = jax.random.bernoulli(key_slow, slow_share, (MIXER_HEADS,))
    fast_rate = jnp.exp(jax.random.uniform(key_fast, (MIXER_HEADS,), jnp.float32, math.log(1.0 / 50.0), math.log(1.0 / 30.0)))
    slow_rate = jnp.exp(jax.random.uniform(key_rate, (MIXER_HEADS,), jnp.float32, math.log(0.1), math.log(0.29))) / PROMPT_TOKENS
    head_rate = jnp.where(slow_heads, slow_rate, fast_rate)
    rough = jax.random.uniform(key_rough, (PROMPT_TOKENS, MIXER_HEADS), jnp.float32, 0.5, 1.5)
    shard_factor = jnp.exp(jax.random.uniform(key_shard, (PROMPT_TOKENS // SHARD_TOKENS, MIXER_HEADS), jnp.float32, math.log(0.6), math.log(1.6)))
    shard_factor = jnp.repeat(shard_factor, SHARD_TOKENS, axis=0)
    baseline_rate = -head_rate[None, :] * rough * shard_factor
    spike_count = 3
    spike_rows = jax.random.randint(key_location, (spike_count,), 0, PROMPT_TOKENS)
    spike_penalty = jax.random.uniform(key_penalty, (spike_count,), jnp.float32, 0.2, 0.4)
    spike_falloff = jnp.zeros((PROMPT_TOKENS,), jnp.float32).at[spike_rows].add(jnp.log1p(-spike_penalty))
    return baseline_rate + spike_falloff[:, None]


def spiked(array, stream_key, source, target, blocks, factor):
    def block_of(axis_at):
        return (jnp.arange(array.shape[axis_at]) // (array.shape[axis_at] // blocks)).reshape((-1,) + (1,) * (array.ndim - 1 - axis_at))

    one_side = jax.random.permutation(stream_key, blocks)[block_of(target)]
    other_side = (block_of(target) + blocks // 2) % blocks
    return jnp.where((block_of(source) == one_side) | (block_of(source) == other_side), factor * array, array)


def levels(stream_key, shape, shards, smallest, high):
    loudness, own = 1.0, jax.random.fold_in(stream_key, 6)
    for dim, shards_of in shards:
        heights = jnp.exp(jax.random.uniform(jax.random.fold_in(own, dim), (shards_of,), jnp.float32, smallest / len(shards), high / len(shards)))
        loudness = loudness * jnp.repeat(heights, shape[dim] // shards_of).reshape([-1 if axis == dim else 1 for axis in range(len(shape))])
    return loudness


def bell_draw(stream_key, extent, deviation, reach, pieces=(), kind=jnp.bfloat16):
    level = levels(stream_key, extent, pieces, -0.22, 0.18) if pieces else 1.0
    values = jax.random.normal(stream_key, extent, jnp.float32) * deviation * level
    return jnp.minimum(jnp.maximum(values, -reach), reach).astype(kind)


def noise_with(key, extent, scale, limit, pieces, heavy, kind=jnp.bfloat16):
    array = scale * jax.random.normal(key, extent, jnp.float32)
    if pieces:
        array = array * levels(key, extent, pieces, -0.22, 0.18)
    return jnp.clip(spiked(array, jax.random.fold_in(key, 3), *heavy), -limit, limit).astype(kind)


def setup_inputs(seed: int = 0) -> dict:
    arg_keys = jax.random.split(jax.random.key(seed), 12)
    queries = draw_queries(jax.random.fold_in(arg_keys[11], 71), 0)
    key_rows = draw_key_rows(jax.random.fold_in(arg_keys[11], 71), 0)
    mixer_input = draw_mixer_input(jax.random.fold_in(arg_keys[11], 71), 0)
    gate_input = bell_draw(arg_keys[3], (PROMPT_TOKENS, MIXER_HEADS * MIXER_CHANNELS), 1.0, 6.0, ((0, 64), (1, 8)))
    write_proj = bell_draw(arg_keys[4], (PROMPT_TOKENS, STATE_SIZE), STATE_SIZE ** -0.5, 0.5, ((0, 64),))
    read_proj = bell_draw(arg_keys[5], (PROMPT_TOKENS, STATE_SIZE), STATE_SIZE ** -0.5, 0.5, ((0, 64),))
    step_size = jnp.clip(jnp.exp(math.log(2.0) - 1.3862944 * jax.random.uniform(arg_keys[6], (PROMPT_TOKENS, MIXER_HEADS), jnp.float32) ** levels(arg_keys[6], (PROMPT_TOKENS, MIXER_HEADS), ((0, 64), (1, 8)), -0.2, 0.2)), 0.5, 2.0)
    log_decay = draw_log_decay(jax.random.fold_in(arg_keys[11], 71), 0)
    skip_gain = jnp.clip(0.5 + 1.5 * jax.random.uniform(arg_keys[8], (MIXER_HEADS,), jnp.float32) ** levels(arg_keys[8], (MIXER_HEADS,), ((0, 8),), -0.2, 0.2), 0.5, 2.0)
    norm_gain = jnp.clip(1.0 + 0.18 * jax.random.normal(arg_keys[9], (MIXER_HEADS * MIXER_CHANNELS,), jnp.float32), 0.1, 1.9)
    value_weight = noise_with(arg_keys[10], (MIXER_HEADS * MIXER_CHANNELS, KEY_HEADS * HEAD_DIM), (MIXER_HEADS * MIXER_CHANNELS) ** -0.5, 0.09375, ((0, 8),), (0, 1, 8, 2.0))
    return {"queries": queries, "key_rows": key_rows, "mixer_input": mixer_input, "gate_input": gate_input, "write_proj": write_proj, "read_proj": read_proj, "step_size": step_size, "log_decay": log_decay, "skip_gain": skip_gain, "norm_gain": norm_gain, "value_weight": value_weight}


rope_base = 10000.0
rope_stretch = 4.0
norm_eps = 1e-05

def rotate(vectors, positions, head_width):
    halfway = head_width // 2
    frequency = rope_base ** (-(2.0 * jnp.arange(halfway, dtype=jnp.float32)) / head_width)
    angles = (positions.astype(jnp.float32) / rope_stretch)[:, None] * frequency[None, :]
    cosine = jnp.cos(angles)[:, None, :]
    sine_part = jnp.sin(angles)[:, None, :]
    front_half = vectors[..., :halfway].astype(jnp.float32)
    back_half = vectors[..., halfway:].astype(jnp.float32)
    turned = jnp.concatenate([front_half * cosine - back_half * sine_part, back_half * cosine + front_half * sine_part], axis=-1)
    return lax.optimization_barrier(turned.astype(jnp.bfloat16))

def attention(queries, key_rows, value_rows):
    token_count = queries.shape[0]
    group_size = QUERY_HEADS // KEY_HEADS
    positions = jnp.arange(token_count, dtype=jnp.int32)
    turned_q = rotate(queries.reshape(token_count, QUERY_HEADS, HEAD_DIM), positions, HEAD_DIM)
    turned_q = turned_q.reshape(token_count, KEY_HEADS, group_size, HEAD_DIM).astype(jnp.float32)
    turned_k = rotate(key_rows.reshape(token_count, KEY_HEADS, HEAD_DIM), positions, HEAD_DIM).astype(jnp.float32)
    value_mat = value_rows.reshape(token_count, KEY_HEADS, HEAD_DIM).astype(jnp.float32)
    block_rows = min(128, token_count)

    def one_block(block_index):
        first_row = block_index * block_rows
        query_block = lax.dynamic_slice_in_dim(turned_q, first_row, block_rows, 0)
        scores = jnp.einsum('tcgd,scd->cgts', query_block, turned_k) * HEAD_DIM ** (-0.5)
        query_pos = first_row + jnp.arange(block_rows, dtype=jnp.int32)
        allowed = positions[None, :] <= query_pos[:, None]
        masked = jnp.where(allowed, scores, -jnp.inf)
        row_max = lax.optimization_barrier(jnp.max(masked, axis=-1, keepdims=True))
        weights = jnp.exp(masked - row_max)
        row_sum = lax.optimization_barrier(jnp.sum(weights, axis=-1))
        rounded = lax.optimization_barrier(weights.astype(jnp.bfloat16)).astype(jnp.float32)
        mixed = jnp.einsum('cgts,scd->tcgd', rounded, value_mat)
        return mixed / jnp.transpose(row_sum, (2, 0, 1))[..., None]
    blocks = lax.map(one_block, jnp.arange(token_count // block_rows, dtype=jnp.int32))
    return blocks.reshape(token_count, QUERY_HEADS * HEAD_DIM).astype(jnp.bfloat16)

def mixer_block(mixer_input, gate_input, write_proj, read_proj, step_size, log_decay, skip_gain, norm_gain):
    token_count = mixer_input.shape[0]
    block_count = token_count // BLOCK_LEN
    shaped_x = mixer_input.reshape(block_count, BLOCK_LEN, MIXER_HEADS, MIXER_CHANNELS)
    shaped_write = write_proj.reshape(block_count, BLOCK_LEN, STATE_SIZE)
    shaped_read = read_proj.reshape(block_count, BLOCK_LEN, STATE_SIZE)
    shaped_step = step_size.reshape(block_count, BLOCK_LEN, MIXER_HEADS)
    shaped_decay = log_decay.reshape(block_count, BLOCK_LEN, MIXER_HEADS)
    causal = (jnp.arange(BLOCK_LEN)[:, None] >= jnp.arange(BLOCK_LEN)[None, :])[:, :, None]

    def advance(carried, items):
        block_x, block_write, block_read, block_step, block_decay = items
        cumul = jnp.cumsum(block_decay, axis=0)
        gram = jnp.dot(block_read, block_write.T, preferred_element_type=jnp.float32)
        spread = cumul[:, None, :] - cumul[None, :, :]
        decay = jnp.where(causal, jnp.exp(jnp.where(causal, spread, 0.0)), 0.0)
        mixing = (decay * gram[:, :, None] * block_step[None, :, :]).astype(jnp.bfloat16)
        mixing = lax.optimization_barrier(mixing).astype(jnp.float32)
        values_full = block_x.astype(jnp.float32)
        intra = jnp.einsum('tsh,shp->thp', mixing, values_full)
        inter = jnp.einsum('tn,hpn->thp', block_read.astype(jnp.float32), carried, precision=lax.Precision.HIGHEST) * jnp.exp(cumul)[:, :, None]
        ending = cumul[-1]
        weighted = (values_full * (block_step * jnp.exp(ending[None, :] - cumul))[:, :, None]).astype(jnp.bfloat16)
        weighted = lax.optimization_barrier(weighted).astype(jnp.float32)
        local_state = jnp.einsum('shp,sn->hpn', weighted, block_write.astype(jnp.float32))
        carried = jnp.exp(ending)[:, None, None] * carried + local_state
        return (carried, intra + inter + skip_gain[None, :, None] * values_full)
    start_state = jnp.zeros((MIXER_HEADS, MIXER_CHANNELS, STATE_SIZE), jnp.float32)
    final_state, outputs = lax.scan(advance, start_state, (shaped_x, shaped_write, shaped_read, shaped_step, shaped_decay))
    outputs = outputs.reshape(token_count, MIXER_HEADS, MIXER_CHANNELS)
    gate_full = gate_input.reshape(token_count, MIXER_HEADS, MIXER_CHANNELS).astype(jnp.float32)
    gated = outputs * jax.nn.silu(gate_full)
    mean_square = lax.optimization_barrier(jnp.mean(gated * gated, axis=(1, 2)))
    normed = gated * lax.rsqrt(mean_square + norm_eps)[:, None, None] * norm_gain.reshape(MIXER_HEADS, MIXER_CHANNELS)
    return normed.reshape(token_count, MIXER_HEADS * MIXER_CHANNELS).astype(jnp.bfloat16)

def reference(queries, key_rows, mixer_input, gate_input, write_proj, read_proj, step_size, log_decay, skip_gain, norm_gain, value_weight):
    mixer_out = mixer_block(mixer_input, gate_input, write_proj, read_proj, step_size, log_decay, skip_gain, norm_gain)
    value_rows = jnp.dot(mixer_out, value_weight, preferred_element_type=jnp.float32).astype(jnp.bfloat16)
    attention_out = attention(queries, key_rows, value_rows)
    return (attention_out, mixer_out)
```

```python
import functools

import jax
import jax.numpy as jnp
import numpy as np
from jax import lax
from jax.experimental import pallas as pl
from jax.experimental.pallas import tpu as pltpu
from jax.sharding import PartitionSpec as P

HEAD_DIM = 128
MIXER_CHANNELS = 64
TOKENS = 128
LANES = 128
ROWS_Y = 4
ROPE_BASE = 10000.0
ROPE_STRETCH = 4.0
NORM_EPS = 1e-05
LOWEST = -1e30
MESH = pl.DeviceIdType.MESH
F32 = jnp.float32
BF16 = jnp.bfloat16
HIGHEST = lax.Precision.HIGHEST
EXP2_SCALE = float(HEAD_DIM**-0.5 * np.log2(np.e))


def dot(a, b, dims=((1,), (0,)), precision=None):
    return lax.dot_general(
        a, b, (dims, ((), ())), precision=precision, preferred_element_type=F32
    )


def kernel(
    ctx_size,
    exp_size,
    q_ref,
    k_ref,
    x_ref,
    gate_ref,
    write_ref,
    read_ref,
    step_ref,
    decay_ref,
    skip_ref,
    gain_ref,
    freq_ref,
    weight_ref,
    attn_ref,
    mixer_ref,
    local_state,
    state_in,
    state_out,
    state_back,
    ends_own,
    ends_all,
    pad_a,
    pad_b,
    decay_rows,
    gated_ref,
    scaled_ref,
    terms_ref,
    terms_in,
    square_own,
    square_in,
    turned_q,
    key_all,
    value_all,
    score_ref,
    prob_ref,
    top_ref,
    sum_ref,
    out_ref,
    a2a_send,
    a2a_recv,
    exp_send,
    exp_recv,
    ring_send,
    key_recv,
    value_recv,
):
    z_size = ctx_size // ROWS_Y
    half = z_size // 2
    heads = step_ref.shape[1]
    pairs = heads // 2
    groups = q_ref.shape[1] // HEAD_DIM
    state_rows = heads * MIXER_CHANNELS // ctx_size
    me = lax.axis_index("ctx")
    col = lax.axis_index("exp")
    my_y = lax.div(me, z_size)
    my_z = lax.rem(me, z_size)

    barrier = pltpu.get_barrier_semaphore()

    def greet_ctx(i, c):
        pl.semaphore_signal(
            barrier, inc=1, device_id={"ctx": lax.rem(me + i, ctx_size)}, device_id_type=MESH
        )
        return c

    lax.fori_loop(1, ctx_size, greet_ctx, 0)

    def greet_exp(i, c):
        pl.semaphore_signal(
            barrier, inc=1, device_id={"exp": lax.rem(col + i, exp_size)}, device_id_type=MESH
        )
        return c

    lax.fori_loop(1, exp_size, greet_exp, 0)

    row = lax.broadcasted_iota(jnp.int32, (TOKENS, LANES), 0)
    lane = lax.broadcasted_iota(jnp.int32, (TOKENS, LANES), 1)
    first = lane < MIXER_CHANNELS
    causal = row >= lane

    def spread(columns, j):
        return jnp.where(first, columns[:, 2 * j : 2 * j + 1], columns[:, 2 * j + 1 : 2 * j + 2])

    position = (me * TOKENS + row).astype(F32)
    angle = (position * (1.0 / ROPE_STRETCH)) * freq_ref[...]
    cosine = jnp.cos(angle)
    sine = jnp.sin(angle)
    sine = jnp.where(first, -sine, sine)

    def turn(v):
        v = v.astype(F32)
        return (v * cosine + pltpu.roll(v, HEAD_DIM // 2, 1) * sine).astype(BF16)

    key_all[me] = turn(k_ref[...])

    tri = jnp.where(causal, 1.0, 0.0).astype(F32)
    cumul = dot(tri, decay_ref[...], precision=HIGHEST)
    ending = cumul[TOKENS - 1 : TOKENS, :]
    ends_own[...] = jnp.zeros_like(ends_own)
    ends_own[0, :, 0:heads] = ending
    ends_all[me] = ends_own[0]
    carry_weight = step_ref[...] * jnp.exp(ending - cumul)
    for j in range(pairs):
        weighted = x_ref[:, j * LANES : (j + 1) * LANES].astype(F32) * spread(carry_weight, j)
        turned = jnp.transpose(weighted).astype(BF16)
        local = dot(turned, write_ref[...]).astype(BF16)
        per = LANES // state_rows
        local_state[j * per : (j + 1) * per] = local.reshape(per, state_rows, LANES)
    state_in[me] = local_state[me]

    pl.semaphore_wait(barrier, ctx_size + exp_size - 2)

    def exchange(source, target, by_peer):
        def one(i, c):
            part, turn_y = lax.div(i, ROWS_Y), lax.rem(lax.rem(i, ROWS_Y) + 1, ROWS_Y)
            odd = lax.rem(part, 2)
            shift = half + (1 - 2 * odd) * lax.div(part + 1, 2)
            peer = lax.rem(my_y + turn_y, ROWS_Y) * z_size + lax.rem(my_z + shift, z_size)
            pltpu.make_async_remote_copy(
                src_ref=source.at[peer if by_peer else 0],
                dst_ref=target.at[me],
                send_sem=a2a_send.at[sem_at[0]],
                recv_sem=a2a_recv.at[sem_at[0]],
                device_id={"ctx": peer},
                device_id_type=MESH,
            ).start()
            return c

        lax.fori_loop(0, ctx_size - 1, one, 0)

    def exchange_wait(target):
        whole = target.at[pl.ds(0, ctx_size - 1)]
        done = pltpu.make_async_remote_copy(
            src_ref=whole,
            dst_ref=whole,
            send_sem=a2a_send.at[sem_at[0]],
            recv_sem=a2a_recv.at[sem_at[0]],
            device_id={"ctx": me},
            device_id_type=MESH,
        )
        done.wait_send()
        done.wait_recv()

    block_b = jnp.where(my_y == 3, 1, 0)
    up_row = jnp.where(my_y == 1, 2, 3)
    right = my_y * z_size + lax.rem(my_z + 1, z_size)
    left = my_y * z_size + lax.rem(my_z + z_size - 1, z_size)

    def push(buffer, recv, index, peer, sem):
        pltpu.make_async_remote_copy(
            src_ref=buffer.at[index],
            dst_ref=buffer.at[index],
            send_sem=sem,
            recv_sem=recv.at[index],
            device_id={"ctx": peer},
            device_id_type=MESH,
        ).start()

    def arrived(buffer, recv, index, sem):
        pltpu.make_async_remote_copy(
            src_ref=buffer.at[index],
            dst_ref=buffer.at[index],
            send_sem=sem,
            recv_sem=recv.at[index],
            device_id={"ctx": me},
            device_id_type=MESH,
        ).wait_recv()

    def ring_open(buffer, recv, sem):
        push(buffer, recv, me, right, sem)
        if half > 1:
            push(buffer, recv, me, left, sem)

        @pl.when(my_y == 0)
        def _():
            push(buffer, recv, me, z_size + my_z, sem)
            push(buffer, recv, me, 2 * z_size + my_z, sem)

        @pl.when(my_y == 1)
        def _():
            push(buffer, recv, me, 3 * z_size + my_z, sem)

        @pl.when(my_y < 3)
        def _():
            push(buffer, recv, me, up_row * z_size + my_z, sem)

    def ring_steps(low, high, buffer, recv, sem, compute):
        def step(s, c):
            @pl.when((s >= 1) & (s <= half))
            def _():
                at = lax.rem(my_z - s + z_size, z_size)
                own = my_y * z_size + at
                arrived(buffer, recv, own, sem)

                @pl.when(s < half)
                def _():
                    push(buffer, recv, own, right, sem)

                @pl.when(my_y < 3)
                def _():
                    push(buffer, recv, own, up_row * z_size + my_z, sem)

            @pl.when((s >= 1) & (s < half))
            def _():
                at = lax.rem(my_z + s, z_size)
                own = my_y * z_size + at
                arrived(buffer, recv, own, sem)

                @pl.when(s < half - 1)
                def _():
                    push(buffer, recv, own, left, sem)

                @pl.when(my_y < 3)
                def _():
                    push(buffer, recv, own, up_row * z_size + my_z, sem)

            @pl.when((my_y > 0) & (s <= half))
            def _():
                at = lax.rem(my_z - s + z_size, z_size)
                other = block_b * z_size + at
                arrived(buffer, recv, other, sem)

                @pl.when(s < half)
                def _():
                    push(buffer, recv, other, right, sem)

                if half > 1:

                    @pl.when(s == 0)
                    def _():
                        push(buffer, recv, other, left, sem)

            @pl.when((my_y > 0) & (s >= 1) & (s < half))
            def _():
                at = lax.rem(my_z + s, z_size)
                other = block_b * z_size + at
                arrived(buffer, recv, other, sem)

                @pl.when(s < half - 1)
                def _():
                    push(buffer, recv, other, left, sem)

            def visit(j, c):
                side, row_y = lax.div(j, ROWS_Y), lax.rem(j, ROWS_Y)
                relayed = (row_y != my_y) & (row_y != block_b) & (row_y < my_y)
                back = s - jnp.where(relayed, 1, 0)
                span = jnp.where(side == 0, back, z_size - back)
                index = row_y * z_size + lax.rem(my_z - span + 2 * z_size, z_size)
                low_ok = back >= side
                high_ok = back <= half - side
                valid = low_ok & high_ok & (row_y <= my_y)

                @pl.when(valid & relayed)
                def _():
                    arrived(buffer, recv, index, sem)

                @pl.when(valid & (index < me))
                def _():
                    compute(index)

                return c

            lax.fori_loop(0, 2 * ROWS_Y, visit, 0)
            return c

        lax.fori_loop(low, high, step, 0)

    ring_total = half + 2

    def ring_close(buffer, sem):
        ring = z_size - 1
        for y, count in enumerate((ring + 2 + z_size, 2 * ring + 1 + z_size, 2 * ring + z_size, 2 * ring)):

            @pl.when(my_y == y)
            def _():
                for part in range(0, count, ctx_size):
                    size = min(ctx_size, count - part)
                    whole = buffer.at[pl.ds(0, size)]
                    pltpu.make_async_remote_copy(
                        src_ref=whole,
                        dst_ref=whole,
                        send_sem=sem,
                        recv_sem=sem,
                        device_id={"ctx": me},
                        device_id_type=MESH,
                    ).wait_send()

    sem_at = [0]
    ring_open(key_all, key_recv, ring_send.at[0])
    exchange(ends_own, ends_all, False)
    sem_at[0] = 1
    exchange(local_state, state_in, True)

    for g in range(groups):
        turned_q[g] = turn(q_ref[:, g * HEAD_DIM : (g + 1) * HEAD_DIM])

    def score(g, index):
        return dot(turned_q[g], key_all[index], ((1,), (1,)))

    for g in range(groups):
        own_score = jnp.where(causal, score(g, me), LOWEST)
        score_ref[me, g] = own_score
        top_ref[g] = own_score

    def key_block(index):
        for g in range(groups):
            s = score(g, index)
            score_ref[index, g] = s
            top_ref[g] = jnp.maximum(top_ref[g], s)

    pad_a[...] = jnp.zeros_like(pad_a)
    pad_b[...] = jnp.zeros_like(pad_b)
    pad_a[:, 0:heads] = cumul
    pad_b[:, 0:heads] = step_ref[...]
    cumul_t = jnp.transpose(pad_a[...])
    step_t = jnp.transpose(pad_b[...])
    gram = dot(read_ref[...], write_ref[...], ((1,), (1,)))
    for j in range(pairs):
        x_pair = x_ref[:, j * LANES : (j + 1) * LANES]
        total = None
        for part in range(2):
            h = 2 * j + part
            exponent = jnp.where(causal, cumul[:, h : h + 1] - cumul_t[h : h + 1, :], LOWEST)
            mixing = (jnp.exp(exponent) * gram * step_t[h : h + 1, :]).astype(BF16)
            keep = first if part == 0 else jnp.logical_not(first)
            term = dot(mixing, jnp.where(keep, x_pair, jnp.zeros_like(x_pair)))
            total = term if total is None else total + term
        skip = jnp.where(
            first[0:1], skip_ref[0:1, 2 * j : 2 * j + 1], skip_ref[0:1, 2 * j + 1 : 2 * j + 2]
        )
        gated_ref[:, j * LANES : (j + 1) * LANES] = total + skip * x_pair.astype(F32)

    split_a, split_b = min(SPLIT[0], ring_total), min(SPLIT[1], ring_total)
    ring_steps(0, split_a, key_all, key_recv, ring_send.at[0], key_block)

    sem_at[0] = 0
    exchange_wait(ends_all)
    head = lax.div(me * state_rows, MIXER_CHANNELS)
    chosen = jnp.where(row == head, 1.0, 0.0).astype(F32)
    decay_rows[...] = jnp.exp(
        dot(ends_all[...].reshape(ctx_size, LANES), chosen, precision=HIGHEST)
    )
    sem_at[0] = 1
    exchange_wait(state_in)

    def scan(b, state):
        state_out[b] = state.astype(BF16)
        return state * decay_rows[pl.ds(b, 1), :] + state_in[b].astype(F32)

    lax.fori_loop(0, ctx_size, scan, jnp.zeros((state_rows, LANES), F32), unroll=8)
    state_back[me] = state_out[me]
    sem_at[0] = 2
    exchange(state_out, state_back, True)

    ring_steps(split_a, split_b, key_all, key_recv, ring_send.at[0], key_block)

    exchange_wait(state_back)
    growth = jnp.exp(cumul)
    squares = jnp.zeros((TOKENS, LANES), F32)
    per = LANES // state_rows
    for j in range(pairs):
        at = slice(j * LANES, (j + 1) * LANES)
        state = state_back[j * per : (j + 1) * per].reshape(LANES, LANES)
        inter = dot(read_ref[...], state, ((1,), (1,))) * spread(growth, j)
        gate = gate_ref[:, at].astype(F32)
        gated = (gated_ref[:, at] + inter) * (gate / (1.0 + jnp.exp(-gate)))
        squares = squares + gated * gated
        scaled = gated * gain_ref[0:1, at]
        gated_ref[:, at] = scaled
        scaled_ref[:, at] = scaled.astype(BF16)
    ones = jnp.ones((8, LANES), F32)
    square_own[0] = dot(ones, squares, ((1,), (1,)), precision=HIGHEST)
    for e in range(exp_size):
        terms = dot(scaled_ref[...], weight_ref[:, e * LANES : (e + 1) * LANES])
        terms_ref[e] = terms.astype(BF16)
    terms_in[col] = terms_ref[col]
    square_in[col] = square_own[0]

    def scatter(i, c):
        peer = lax.rem(col + i, exp_size)
        pltpu.make_async_remote_copy(
            src_ref=square_own.at[0],
            dst_ref=square_in.at[col],
            send_sem=exp_send.at[0],
            recv_sem=exp_recv.at[0],
            device_id={"exp": peer},
            device_id_type=MESH,
        ).start()
        pltpu.make_async_remote_copy(
            src_ref=terms_ref.at[peer],
            dst_ref=terms_in.at[col],
            send_sem=exp_send.at[1],
            recv_sem=exp_recv.at[1],
            device_id={"exp": peer},
            device_id_type=MESH,
        ).start()
        return c

    lax.fori_loop(1, exp_size, scatter, 0)

    ring_steps(split_b, ring_total, key_all, key_recv, ring_send.at[0], key_block)
    ring_close(key_all, ring_send.at[0])

    for g in range(groups):
        top_ref[g] = jnp.broadcast_to(jnp.max(top_ref[g], axis=1, keepdims=True), (TOKENS, LANES))
        sum_ref[g] = jnp.zeros((TOKENS, LANES), F32)
        out_ref[g] = jnp.zeros((TOKENS, LANES), F32)

    def weigh(b, c):
        for g in range(groups):
            p = jnp.exp2((score_ref[b, g] - top_ref[g]) * EXP2_SCALE)
            sum_ref[g] += p
            prob_ref[b, g] = p.astype(BF16)
        return c

    lax.fori_loop(0, me + 1, weigh, 0)

    for slot, target in ((0, square_in), (1, terms_in)):
        whole = target.at[pl.ds(0, exp_size - 1)]
        done = pltpu.make_async_remote_copy(
            src_ref=whole,
            dst_ref=whole,
            send_sem=exp_send.at[slot],
            recv_sem=exp_recv.at[slot],
            device_id={"exp": col},
            device_id_type=MESH,
        )
        done.wait_send()
        done.wait_recv()
    square_row = square_in[0]
    for e in range(1, exp_size):
        square_row = square_row + square_in[e]
    square = jnp.transpose(jnp.broadcast_to(square_row[0:1, :], (TOKENS, LANES)))
    factor = lax.rsqrt(square * (1.0 / (exp_size * heads * MIXER_CHANNELS)) + NORM_EPS)
    value = terms_in[0].astype(F32)
    for e in range(1, exp_size):
        value = value + terms_in[e].astype(F32)
    value_all[me] = (value * factor).astype(BF16)
    ring_open(value_all, value_recv, ring_send.at[1])

    for j in range(pairs):
        at = slice(j * LANES, (j + 1) * LANES)
        mixer_ref[:, at] = (gated_ref[:, at] * factor).astype(BF16)

    def value_block(index):
        for g in range(groups):
            out_ref[g] += dot(prob_ref[index, g], value_all[index])

    value_block(me)
    ring_steps(0, ring_total, value_all, value_recv, ring_send.at[1], value_block)
    for g in range(groups):
        total = jnp.sum(sum_ref[g], axis=1, keepdims=True)
        attn_ref[:, g * HEAD_DIM : (g + 1) * HEAD_DIM] = (out_ref[g] / total).astype(BF16)
    ring_close(value_all, ring_send.at[1])


SPLIT = (4, 8)


def solution(mesh):
    ctx_size, exp_size = mesh.shape["ctx"], mesh.shape["exp"]

    def on_device(
        queries,
        key_rows,
        mixer_input,
        gate_input,
        write_proj,
        read_proj,
        step_size,
        log_decay,
        skip_gain,
        norm_gain,
        value_weight,
    ):
        heads = step_size.shape[1]
        channels = heads * MIXER_CHANNELS
        groups = queries.shape[1] // HEAD_DIM
        state_rows = channels // ctx_size
        frequency = ROPE_BASE ** (-(2.0 * np.arange(HEAD_DIM // 2)) / HEAD_DIM)
        frequency = jnp.asarray(np.tile(frequency, 2)[None, :], F32)
        vmem = functools.partial(pl.BlockSpec, memory_space=pltpu.VMEM)
        tile = (TOKENS, LANES)
        return pl.pallas_call(
            functools.partial(kernel, ctx_size, exp_size),
            out_shape=(
                jax.ShapeDtypeStruct(queries.shape, BF16),
                jax.ShapeDtypeStruct(mixer_input.shape, BF16),
            ),
            in_specs=[vmem()] * 12,
            out_specs=(vmem(), vmem()),
            scratch_shapes=[
                pltpu.VMEM((ctx_size, state_rows, LANES), BF16),
                pltpu.VMEM((ctx_size, state_rows, LANES), BF16),
                pltpu.VMEM((ctx_size, state_rows, LANES), BF16),
                pltpu.VMEM((ctx_size, state_rows, LANES), BF16),
                pltpu.VMEM((1, 1, LANES), F32),
                pltpu.VMEM((ctx_size, 1, LANES), F32),
                pltpu.VMEM(tile, F32),
                pltpu.VMEM(tile, F32),
                pltpu.VMEM((ctx_size, LANES), F32),
                pltpu.VMEM((TOKENS, channels), F32),
                pltpu.VMEM((TOKENS, channels), BF16),
                pltpu.VMEM((exp_size,) + tile, BF16),
                pltpu.VMEM((exp_size,) + tile, BF16),
                pltpu.VMEM((1, 8, LANES), F32),
                pltpu.VMEM((exp_size, 8, LANES), F32),
                pltpu.VMEM((groups,) + tile, BF16),
                pltpu.VMEM((ctx_size,) + tile, BF16),
                pltpu.VMEM((ctx_size,) + tile, BF16),
                pltpu.VMEM((ctx_size, groups) + tile, F32),
                pltpu.VMEM((ctx_size, groups) + tile, BF16),
                pltpu.VMEM((groups,) + tile, F32),
                pltpu.VMEM((groups,) + tile, F32),
                pltpu.VMEM((groups,) + tile, F32),
                pltpu.SemaphoreType.DMA((3,)),
                pltpu.SemaphoreType.DMA((3,)),
                pltpu.SemaphoreType.DMA((2,)),
                pltpu.SemaphoreType.DMA((2,)),
                pltpu.SemaphoreType.DMA((2,)),
                pltpu.SemaphoreType.DMA((ctx_size,)),
                pltpu.SemaphoreType.DMA((ctx_size,)),
            ],
            compiler_params=pltpu.CompilerParams(
                collective_id=0, has_side_effects=True, vmem_limit_bytes=56 * 1024 * 1024
            ),
        )(
            queries,
            key_rows,
            mixer_input,
            gate_input,
            write_proj,
            read_proj,
            step_size,
            log_decay,
            skip_gain.reshape(1, heads),
            norm_gain.reshape(1, channels),
            frequency,
            value_weight,
        )

    return jax.shard_map(
        on_device,
        mesh=mesh,
        in_specs=(
            P("ctx", "exp"),
            P("ctx", "exp"),
            P("ctx", "exp"),
            P("ctx", "exp"),
            P("ctx", None),
            P("ctx", None),
            P("ctx", "exp"),
            P("ctx", "exp"),
            P("exp"),
            P("exp"),
            P("exp", None),
        ),
        out_specs=(P("ctx", "exp"), P("ctx", "exp")),
        check_vma=False,
    )
```

```python
import functools

import jax
import jax.numpy as jnp
import numpy as np
from jax import lax
from jax.experimental import pallas as pl
from jax.experimental.pallas import tpu as pltpu
from jax.sharding import PartitionSpec as P

HEAD_DIM = 128
MIXER_CHANNELS = 64
TOKENS = 128
LANES = 128
ROWS_Y = 4
ROPE_BASE = 10000.0
ROPE_STRETCH = 4.0
NORM_EPS = 1e-05
LOWEST = -1e30
MESH = pl.DeviceIdType.MESH
F32 = jnp.float32
BF16 = jnp.bfloat16
HIGHEST = lax.Precision.HIGHEST
EXP2_SCALE = float(HEAD_DIM**-0.5 * np.log2(np.e))


def dot(a, b, dims=((1,), (0,)), precision=None):
    return lax.dot_general(
        a, b, (dims, ((), ())), precision=precision, preferred_element_type=F32
    )


def kernel(
    ctx_size,
    exp_size,
    *refs,
):
    inputs, refs = refs[:INPUTS], refs[INPUTS:]
    attn_out, mixer_out = refs[:2]
    staged, refs = refs[2 : 2 + INPUTS], refs[2 + INPUTS :]
    (
        k_ref,
        decay_ref,
        step_ref,
        freq_ref,
        x_ref,
        write_ref,
        read_ref,
        q_ref,
        skip_ref,
        gate_ref,
        gain_ref,
        weight_ref,
    ) = staged
    (
    attn_ref,
    mixer_ref,
    load_sem,
    store_sem,
    local_state,
    state_in,
    state_out,
    state_back,
    ends_own,
    ends_all,
    pad_a,
    pad_b,
    decay_rows,
    gated_ref,
    scaled_ref,
    terms_ref,
    terms_in,
    square_own,
    square_in,
    turned_q,
    key_all,
    value_all,
    score_ref,
    prob_ref,
    top_ref,
    sum_ref,
    out_ref,
    a2a_send,
    a2a_recv,
    exp_send,
    exp_recv,
    ring_send,
    key_recv,
    value_recv,
    ) = refs
    z_size = ctx_size // ROWS_Y
    half = z_size // 2
    heads = step_ref.shape[0]
    pairs = heads // 2
    groups = q_ref.shape[1] // HEAD_DIM
    state_rows = heads * MIXER_CHANNELS // ctx_size
    me = lax.axis_index("ctx")
    col = lax.axis_index("exp")
    my_y = lax.div(me, z_size)
    my_z = lax.rem(me, z_size)

    barrier = pltpu.get_barrier_semaphore()

    def peer_of(i):
        part, turn_y = lax.div(i, ROWS_Y), lax.rem(lax.rem(i, ROWS_Y) + 1, ROWS_Y)
        odd = lax.rem(part, 2)
        shift = half + (1 - 2 * odd) * lax.div(part + 1, 2)
        return lax.rem(my_y + turn_y, ROWS_Y) * z_size + lax.rem(my_z + shift, z_size)

    def greet_ctx(i, c):
        pl.semaphore_signal(
            barrier, inc=1, device_id={"ctx": peer_of(i)}, device_id_type=MESH
        )
        return c

    lax.fori_loop(0, ctx_size - 1, greet_ctx, 0, unroll=UNROLL)

    def greet_exp(i, c):
        pl.semaphore_signal(
            barrier, inc=1, device_id={"exp": lax.rem(col + i, exp_size)}, device_id_type=MESH
        )
        return c

    lax.fori_loop(1, exp_size, greet_exp, 0)
    loads = [
        pltpu.make_async_copy(a, b, load_sem.at[i]) for i, (a, b) in enumerate(zip(inputs, staged))
    ]
    for load in loads:
        load.start()
    pad_a[...] = jnp.zeros_like(pad_a)
    pad_b[...] = jnp.zeros_like(pad_b)
    for load in loads[:4]:
        load.wait()

    row = lax.broadcasted_iota(jnp.int32, (TOKENS, LANES), 0)
    lane = lax.broadcasted_iota(jnp.int32, (TOKENS, LANES), 1)
    first = lane < MIXER_CHANNELS
    causal = row >= lane

    def spread(columns, j):
        return jnp.where(first, columns[:, 2 * j : 2 * j + 1], columns[:, 2 * j + 1 : 2 * j + 2])

    position = (me * TOKENS + row).astype(F32)
    angle = (position * (1.0 / ROPE_STRETCH)) * freq_ref[...]
    cosine = jnp.cos(angle)
    sine = jnp.sin(angle)
    sine = jnp.where(first, -sine, sine)

    def turn(v):
        v = v.astype(F32)
        return (v * cosine + pltpu.roll(v, HEAD_DIM // 2, 1) * sine).astype(BF16)

    key_all[me] = turn(k_ref[...])

    tri = jnp.where(row <= lane, 1.0, 0.0).astype(F32)
    cumul_t = dot(decay_ref[...], tri, precision=HIGHEST)
    pad_a[0:heads, :] = cumul_t
    pad_b[0:heads, :] = step_ref[...]
    cumul = jnp.transpose(pad_a[...])
    ending = cumul[TOKENS - 1 : TOKENS, :]
    ends_own[0] = ending
    ends_all[me] = ending
    carry_weight = jnp.transpose(pad_b[...]) * jnp.exp(ending - cumul)
    for load in loads[4:6]:
        load.wait()
    for j in range(pairs):
        weighted = x_ref[:, j * LANES : (j + 1) * LANES].astype(F32) * spread(carry_weight, j)
        turned = jnp.transpose(weighted).astype(BF16)
        local = dot(turned, write_ref[...]).astype(BF16)
        per = LANES // state_rows
        local_state[j * per : (j + 1) * per] = local.reshape(per, state_rows, LANES)
    state_in[me] = local_state[me]

    pl.semaphore_wait(barrier, ctx_size + exp_size - 2)

    def exchange(*moves):
        def one(i, c):
            peer = peer_of(i)
            for slot, source, target in moves:
                pltpu.make_async_remote_copy(
                    src_ref=source.at[peer if slot else 0],
                    dst_ref=target.at[me],
                    send_sem=a2a_send.at[slot],
                    recv_sem=a2a_recv.at[slot],
                    device_id={"ctx": peer},
                    device_id_type=MESH,
                ).start()
            return c

        lax.fori_loop(0, ctx_size - 1, one, 0, unroll=UNROLL)

    def exchange_wait(slot, target):
        whole = target.at[pl.ds(0, ctx_size - 1)]
        done = pltpu.make_async_remote_copy(
            src_ref=whole,
            dst_ref=whole,
            send_sem=a2a_send.at[slot],
            recv_sem=a2a_recv.at[slot],
            device_id={"ctx": me},
            device_id_type=MESH,
        )
        done.wait_send()
        done.wait_recv()

    key_length, value_length = half // SEGMENTS[0], half // SEGMENTS[1]
    block_b = jnp.where(my_y == 3, 1, 0)
    up_row = jnp.where(my_y == 1, 2, 3)
    right = my_y * z_size + lax.rem(my_z + 1, z_size)
    left = my_y * z_size + lax.rem(my_z + z_size - 1, z_size)

    def push(buffer, recv, index, peer, sem):
        pltpu.make_async_remote_copy(
            src_ref=buffer.at[index],
            dst_ref=buffer.at[index],
            send_sem=sem,
            recv_sem=recv.at[index],
            device_id={"ctx": peer},
            device_id_type=MESH,
        ).start()

    def arrived(buffer, recv, index, sem):
        pltpu.make_async_remote_copy(
            src_ref=buffer.at[index],
            dst_ref=buffer.at[index],
            send_sem=sem,
            recv_sem=recv.at[index],
            device_id={"ctx": me},
            device_id_type=MESH,
        ).wait_recv()

    def at_distance(d):
        return lax.rem(my_z + d + 2 * z_size, z_size)

    def launch(buffer, recv, sem, length, index):
        for d in reversed(range(1, half + 1, length)):
            push(buffer, recv, index, my_y * z_size + at_distance(d), sem)
            if d < half:
                push(buffer, recv, index, my_y * z_size + at_distance(-d), sem)

    def ring_open(buffer, recv, sem, length):
        @pl.when(my_y == 0)
        def _():
            push(buffer, recv, me, z_size + my_z, sem)
            push(buffer, recv, me, 2 * z_size + my_z, sem)

        @pl.when(my_y == 1)
        def _():
            push(buffer, recv, me, 3 * z_size + my_z, sem)

        launch(buffer, recv, sem, length, me)

        @pl.when(my_y < 3)
        def _():
            push(buffer, recv, me, up_row * z_size + my_z, sem)

    def ring_steps(low, high, buffer, recv, sem, length, compute):
        segments = half // length

        def step(s, c):
            moving = (s >= 1) & (s <= length)

            for source, lifted in ((my_y, True), (block_b, False)):
                ready = moving if lifted else moving & (my_y > 0)
                if not lifted:

                    @pl.when((s == 0) & (my_y > 0))
                    def _():
                        index = block_b * z_size + my_z
                        arrived(buffer, recv, index, sem)
                        launch(buffer, recv, sem, length, index)

                for segment in range(segments):
                    for side in range(2):
                        d = s + segment * length

                        @pl.when(ready & (d <= half - side))
                        def _():
                            index = source * z_size + at_distance(d if side else -d)
                            arrived(buffer, recv, index, sem)

                            @pl.when((s < length) & (d < half - side))
                            def _():
                                push(buffer, recv, index, left if side else right, sem)

                            if lifted:

                                @pl.when(my_y < 3)
                                def _():
                                    push(buffer, recv, index, up_row * z_size + my_z, sem)

            def visit(j, c):
                segment, rest = lax.div(j, 2 * ROWS_Y), lax.rem(j, 2 * ROWS_Y)
                side, row_y = lax.div(rest, ROWS_Y), lax.rem(rest, ROWS_Y)
                relayed = (row_y != my_y) & (row_y != block_b) & (row_y < my_y)
                back = s - jnp.where(relayed, 1, 0)
                d = back + segment * length
                index = row_y * z_size + at_distance(jnp.where(side == 0, -d, d))
                fits = (back <= length) & (d <= half - side)
                starts = (back >= 1) | ((back == 0) & (segment == 0) & (side == 0))
                valid = fits & starts & (row_y <= my_y)

                @pl.when(valid & relayed)
                def _():
                    arrived(buffer, recv, index, sem)

                @pl.when(valid & (index < me))
                def _():
                    compute(index)

                return c

            lax.fori_loop(0, segments * 2 * ROWS_Y, visit, 0)
            return c

        lax.fori_loop(low, high, step, 0)

    def ring_close(buffer, sem):
        ring = z_size - 1
        for y, count in enumerate((ring + 2 + z_size, 2 * ring + 1 + z_size, 2 * ring + z_size, 2 * ring)):

            @pl.when(my_y == y)
            def _():
                for part in range(0, count, ctx_size):
                    size = min(ctx_size, count - part)
                    whole = buffer.at[pl.ds(0, size)]
                    pltpu.make_async_remote_copy(
                        src_ref=whole,
                        dst_ref=whole,
                        send_sem=sem,
                        recv_sem=sem,
                        device_id={"ctx": me},
                        device_id_type=MESH,
                    ).wait_send()

    ring_open(key_all, key_recv, ring_send.at[0], key_length)
    exchange((1, local_state, state_in), (0, ends_own, ends_all))
    for load in loads[6:]:
        load.wait()

    for g in range(groups):
        turned_q[g] = turn(q_ref[:, g * HEAD_DIM : (g + 1) * HEAD_DIM])

    def score(index):
        return dot(turned_q[...].reshape(groups * TOKENS, LANES), key_all[index], ((1,), (1,)))

    own_score = score(me)
    for g in range(groups):
        masked = jnp.where(causal, own_score[g * TOKENS : (g + 1) * TOKENS], LOWEST)
        score_ref[me, g] = masked
        top_ref[g] = masked

    def key_block(index):
        s = score(index).reshape(groups, TOKENS, LANES)
        score_ref[index] = s
        top_ref[...] = jnp.maximum(top_ref[...], s)

    gram = dot(read_ref[...], write_ref[...], ((1,), (1,)))
    for j in range(pairs):
        x_pair = x_ref[:, j * LANES : (j + 1) * LANES]
        total = None
        for part in range(2):
            h = 2 * j + part
            exponent = jnp.where(causal, cumul[:, h : h + 1] - cumul_t[h : h + 1, :], LOWEST)
            mixing = (jnp.exp(exponent) * gram * step_ref[h : h + 1, :]).astype(BF16)
            keep = first if part == 0 else jnp.logical_not(first)
            term = dot(mixing, jnp.where(keep, x_pair, jnp.zeros_like(x_pair)))
            total = term if total is None else total + term
        skip = jnp.where(
            first[0:1], skip_ref[0:1, 2 * j : 2 * j + 1], skip_ref[0:1, 2 * j + 1 : 2 * j + 2]
        )
        gated_ref[:, j * LANES : (j + 1) * LANES] = total + skip * x_pair.astype(F32)

    split_a, split_b = min(SPLIT[0], key_length + 2), min(SPLIT[1], key_length + 2)
    ring_steps(0, split_a, key_all, key_recv, ring_send.at[0], key_length, key_block)

    exchange_wait(0, ends_all)
    head = lax.div(me * state_rows, MIXER_CHANNELS)
    chosen = jnp.where(row == head, 1.0, 0.0).astype(F32)
    decay_rows[...] = jnp.exp(
        dot(ends_all[...].reshape(ctx_size, LANES), chosen, precision=HIGHEST)
    )
    exchange_wait(1, state_in)

    def scan(b, state):
        state_out[b] = state.astype(BF16)
        return state * decay_rows[pl.ds(b, 1), :] + state_in[b].astype(F32)

    lax.fori_loop(0, ctx_size, scan, jnp.zeros((state_rows, LANES), F32), unroll=8)
    state_back[me] = state_out[me]
    exchange((2, state_out, state_back))

    ring_steps(split_a, split_b, key_all, key_recv, ring_send.at[0], key_length, key_block)

    exchange_wait(2, state_back)
    growth = jnp.exp(cumul)
    squares = jnp.zeros((TOKENS, LANES), F32)
    per = LANES // state_rows
    for j in range(pairs):
        at = slice(j * LANES, (j + 1) * LANES)
        state = state_back[j * per : (j + 1) * per].reshape(LANES, LANES)
        inter = dot(read_ref[...], state, ((1,), (1,))) * spread(growth, j)
        gate = gate_ref[:, at].astype(F32)
        gated = (gated_ref[:, at] + inter) * (gate / (1.0 + jnp.exp(-gate)))
        squares = squares + gated * gated
        scaled = gated * gain_ref[0:1, at]
        gated_ref[:, at] = scaled
        scaled_ref[:, at] = scaled.astype(BF16)
    ones = jnp.ones((8, LANES), F32)
    square_own[0] = dot(ones, squares, ((1,), (1,)), precision=HIGHEST)
    for e in range(exp_size):
        terms = dot(scaled_ref[...], weight_ref[:, e * LANES : (e + 1) * LANES])
        terms_ref[e] = terms.astype(BF16)
    terms_in[col] = terms_ref[col]
    square_in[col] = square_own[0]

    def scatter(i, c):
        peer = lax.rem(col + i, exp_size)
        pltpu.make_async_remote_copy(
            src_ref=square_own.at[0],
            dst_ref=square_in.at[col],
            send_sem=exp_send.at[0],
            recv_sem=exp_recv.at[0],
            device_id={"exp": peer},
            device_id_type=MESH,
        ).start()
        pltpu.make_async_remote_copy(
            src_ref=terms_ref.at[peer],
            dst_ref=terms_in.at[col],
            send_sem=exp_send.at[1],
            recv_sem=exp_recv.at[1],
            device_id={"exp": peer},
            device_id_type=MESH,
        ).start()
        return c

    lax.fori_loop(1, exp_size, scatter, 0)

    ring_steps(split_b, key_length + 2, key_all, key_recv, ring_send.at[0], key_length, key_block)
    ring_close(key_all, ring_send.at[0])

    for g in range(groups):
        top_ref[g] = jnp.broadcast_to(jnp.max(top_ref[g], axis=1, keepdims=True), (TOKENS, LANES))
        sum_ref[g] = jnp.zeros((TOKENS, LANES), F32)
        out_ref[g] = jnp.zeros((TOKENS, LANES), F32)

    def weigh(b, c):
        for g in range(groups):
            p = jnp.exp2((score_ref[b, g] - top_ref[g]) * EXP2_SCALE)
            sum_ref[g] += p
            prob_ref[b, g] = p.astype(BF16)
        return c

    lax.fori_loop(0, me + 1, weigh, 0)

    for slot, target in ((0, square_in), (1, terms_in)):
        whole = target.at[pl.ds(0, exp_size - 1)]
        done = pltpu.make_async_remote_copy(
            src_ref=whole,
            dst_ref=whole,
            send_sem=exp_send.at[slot],
            recv_sem=exp_recv.at[slot],
            device_id={"exp": col},
            device_id_type=MESH,
        )
        done.wait_send()
        done.wait_recv()
    square_row = square_in[0]
    for e in range(1, exp_size):
        square_row = square_row + square_in[e]
    square = jnp.transpose(jnp.broadcast_to(square_row[0:1, :], (TOKENS, LANES)))
    factor = lax.rsqrt(square * (1.0 / (exp_size * heads * MIXER_CHANNELS)) + NORM_EPS)
    value = terms_in[0].astype(F32)
    for e in range(1, exp_size):
        value = value + terms_in[e].astype(F32)
    value_all[me] = (value * factor).astype(BF16)
    ring_open(value_all, value_recv, ring_send.at[1], value_length)

    for j in range(pairs):
        at = slice(j * LANES, (j + 1) * LANES)
        mixer_ref[:, at] = (gated_ref[:, at] * factor).astype(BF16)

    store_mixer = pltpu.make_async_copy(mixer_ref, mixer_out, store_sem.at[0])
    store_mixer.start()

    def value_block(index):
        probs = prob_ref[index].reshape(groups * TOKENS, LANES)
        out_ref[...] += dot(probs, value_all[index]).reshape(groups, TOKENS, LANES)

    value_block(me)
    ring_steps(
        0, value_length + 2, value_all, value_recv, ring_send.at[1], value_length, value_block
    )
    for g in range(groups):
        total = jnp.sum(sum_ref[g], axis=1, keepdims=True)
        attn_ref[:, g * HEAD_DIM : (g + 1) * HEAD_DIM] = (out_ref[g] / total).astype(BF16)
    store_attn = pltpu.make_async_copy(attn_ref, attn_out, store_sem.at[1])
    store_attn.start()
    ring_close(value_all, ring_send.at[1])
    store_mixer.wait()
    store_attn.wait()


def hand_over(attn_in, mixer_in, attn_out, mixer_out, sem):
    first = pltpu.make_async_copy(attn_in, attn_out, sem.at[0])
    second = pltpu.make_async_copy(mixer_in, mixer_out, sem.at[1])
    first.start()
    second.start()
    first.wait()
    second.wait()


SPLIT = (2, 6)
SEGMENTS = (1, 2)
INPUTS = 12
UNROLL = 7


def solution(mesh):
    ctx_size, exp_size = mesh.shape["ctx"], mesh.shape["exp"]

    def on_device(
        queries,
        key_rows,
        mixer_input,
        gate_input,
        write_proj,
        read_proj,
        step_size,
        log_decay,
        skip_gain,
        norm_gain,
        value_weight,
    ):
        heads = step_size.shape[1]
        channels = heads * MIXER_CHANNELS
        groups = queries.shape[1] // HEAD_DIM
        state_rows = channels // ctx_size
        frequency = ROPE_BASE ** (-(2.0 * np.arange(HEAD_DIM // 2)) / HEAD_DIM)
        frequency = jnp.asarray(np.tile(frequency, 2)[None, :], F32)
        tile = (TOKENS, LANES)
        anywhere = pl.BlockSpec(memory_space=pl.ANY)
        operands = (
            key_rows,
            log_decay.T,
            step_size.T,
            frequency,
            mixer_input,
            write_proj,
            read_proj,
            queries,
            skip_gain.reshape(1, heads),
            gate_input,
            norm_gain.reshape(1, channels),
            value_weight,
        )
        results = (
            jax.ShapeDtypeStruct(queries.shape, BF16),
            jax.ShapeDtypeStruct(mixer_input.shape, BF16),
        )
        staged = [pltpu.VMEM(a.shape, a.dtype) for a in operands]
        held = [pltpu.VMEM(a.shape, a.dtype) for a in results]
        found = pl.pallas_call(
            functools.partial(kernel, ctx_size, exp_size),
            out_shape=results,
            in_specs=[anywhere] * INPUTS,
            out_specs=(anywhere, anywhere),
            scratch_shapes=staged
            + held
            + [
                pltpu.SemaphoreType.DMA((INPUTS,)),
                pltpu.SemaphoreType.DMA((2,)),
                pltpu.VMEM((ctx_size, state_rows, LANES), BF16),
                pltpu.VMEM((ctx_size, state_rows, LANES), BF16),
                pltpu.VMEM((ctx_size, state_rows, LANES), BF16),
                pltpu.VMEM((ctx_size, state_rows, LANES), BF16),
                pltpu.VMEM((1, 1, LANES), F32),
                pltpu.VMEM((ctx_size, 1, LANES), F32),
                pltpu.VMEM(tile, F32),
                pltpu.VMEM(tile, F32),
                pltpu.VMEM((ctx_size, LANES), F32),
                pltpu.VMEM((TOKENS, channels), F32),
                pltpu.VMEM((TOKENS, channels), BF16),
                pltpu.VMEM((exp_size,) + tile, BF16),
                pltpu.VMEM((exp_size,) + tile, BF16),
                pltpu.VMEM((1, 8, LANES), F32),
                pltpu.VMEM((exp_size, 8, LANES), F32),
                pltpu.VMEM((groups,) + tile, BF16),
                pltpu.VMEM((ctx_size,) + tile, BF16),
                pltpu.VMEM((ctx_size,) + tile, BF16),
                pltpu.VMEM((ctx_size, groups) + tile, F32),
                pltpu.VMEM((ctx_size, groups) + tile, BF16),
                pltpu.VMEM((groups,) + tile, F32),
                pltpu.VMEM((groups,) + tile, F32),
                pltpu.VMEM((groups,) + tile, F32),
                pltpu.SemaphoreType.DMA((3,)),
                pltpu.SemaphoreType.DMA((3,)),
                pltpu.SemaphoreType.DMA((2,)),
                pltpu.SemaphoreType.DMA((2,)),
                pltpu.SemaphoreType.DMA((2,)),
                pltpu.SemaphoreType.DMA((ctx_size,)),
                pltpu.SemaphoreType.DMA((ctx_size,)),
            ],
            compiler_params=pltpu.CompilerParams(
                collective_id=0, has_side_effects=True, vmem_limit_bytes=56 * 1024 * 1024
            ),
        )(*operands)
        return pl.pallas_call(
            hand_over,
            out_shape=results,
            in_specs=[pl.BlockSpec(memory_space=pltpu.VMEM)] * 2,
            out_specs=(anywhere, anywhere),
            scratch_shapes=[pltpu.SemaphoreType.DMA((2,))],
            compiler_params=pltpu.CompilerParams(vmem_limit_bytes=2 * 1024 * 1024),
        )(*found)

    return jax.shard_map(
        on_device,
        mesh=mesh,
        in_specs=(
            P("ctx", "exp"),
            P("ctx", "exp"),
            P("ctx", "exp"),
            P("ctx", "exp"),
            P("ctx", None),
            P("ctx", None),
            P("ctx", "exp"),
            P("ctx", "exp"),
            P("exp"),
            P("exp"),
            P("exp", None),
        ),
        out_specs=(P("ctx", "exp"), P("ctx", "exp")),
        check_vma=False,
    )
```

```python
import functools

import jax
import jax.numpy as jnp
import numpy as np
from jax import lax
from jax.experimental import pallas as pl
from jax.experimental.pallas import tpu as pltpu
from jax.sharding import PartitionSpec as P

HEAD_DIM = 128
MIXER_CHANNELS = 64
TOKENS = 128
LANES = 128
ROWS_Y = 4
ROPE_BASE = 10000.0
ROPE_STRETCH = 4.0
NORM_EPS = 1e-05
LOWEST = -1e30
MESH = pl.DeviceIdType.MESH
F32 = jnp.float32
BF16 = jnp.bfloat16
HIGHEST = lax.Precision.HIGHEST
EXP2_SCALE = float(HEAD_DIM**-0.5 * np.log2(np.e))


def dot(a, b, dims=((1,), (0,)), precision=None):
    return lax.dot_general(
        a, b, (dims, ((), ())), precision=precision, preferred_element_type=F32
    )


def kernel(
    ctx_size,
    exp_size,
    *refs,
):
    inputs, refs = refs[:INPUTS], refs[INPUTS:]
    attn_ref, mixer_ref = refs[:2]
    staged, refs = refs[2 : 2 + INPUTS], refs[2 + INPUTS :]
    (
        k_ref,
        decay_ref,
        step_ref,
        freq_ref,
        x_ref,
        write_ref,
        read_ref,
        q_ref,
        skip_ref,
        gate_ref,
        gain_ref,
        weight_ref,
    ) = staged
    (
    load_sem,
    local_state,
    state_in,
    state_out,
    state_back,
    ends_own,
    ends_all,
    pad_a,
    pad_b,
    decay_rows,
    gated_ref,
    scaled_ref,
    terms_ref,
    terms_in,
    square_own,
    square_in,
    turned_q,
    key_all,
    value_all,
    score_ref,
    prob_ref,
    top_ref,
    sum_ref,
    out_ref,
    a2a_send,
    a2a_recv,
    exp_send,
    exp_recv,
    ring_send,
    key_recv,
    value_recv,
    ) = refs
    z_size = ctx_size // ROWS_Y
    half = z_size // 2
    heads = step_ref.shape[0]
    pairs = heads // 2
    groups = q_ref.shape[1] // HEAD_DIM
    state_rows = heads * MIXER_CHANNELS // ctx_size
    me = lax.axis_index("ctx")
    col = lax.axis_index("exp")
    my_y = lax.div(me, z_size)
    my_z = lax.rem(me, z_size)

    barrier = pltpu.get_barrier_semaphore()

    def peer_of(i):
        part, turn_y = lax.div(i, ROWS_Y), lax.rem(lax.rem(i, ROWS_Y) + 1, ROWS_Y)
        odd = lax.rem(part, 2)
        shift = half + (1 - 2 * odd) * lax.div(part + 1, 2)
        return lax.rem(my_y + turn_y, ROWS_Y) * z_size + lax.rem(my_z + shift, z_size)

    def greet_ctx(i, c):
        pl.semaphore_signal(
            barrier, inc=1, device_id={"ctx": peer_of(i)}, device_id_type=MESH
        )
        return c

    lax.fori_loop(0, ctx_size - 1, greet_ctx, 0, unroll=UNROLL)

    def greet_exp(i, c):
        pl.semaphore_signal(
            barrier, inc=1, device_id={"exp": lax.rem(col + i, exp_size)}, device_id_type=MESH
        )
        return c

    lax.fori_loop(1, exp_size, greet_exp, 0)
    loads = [
        pltpu.make_async_copy(a, b, load_sem.at[i]) for i, (a, b) in enumerate(zip(inputs, staged))
    ]
    for load in loads:
        load.start()
    pad_a[...] = jnp.zeros_like(pad_a)
    pad_b[...] = jnp.zeros_like(pad_b)
    for load in loads[:4]:
        load.wait()

    row = lax.broadcasted_iota(jnp.int32, (TOKENS, LANES), 0)
    lane = lax.broadcasted_iota(jnp.int32, (TOKENS, LANES), 1)
    first = lane < MIXER_CHANNELS
    causal = row >= lane

    def spread(columns, j):
        return jnp.where(first, columns[:, 2 * j : 2 * j + 1], columns[:, 2 * j + 1 : 2 * j + 2])

    position = (me * TOKENS + row).astype(F32)
    angle = (position * (1.0 / ROPE_STRETCH)) * freq_ref[...]
    cosine = jnp.cos(angle)
    sine = jnp.sin(angle)
    sine = jnp.where(first, -sine, sine)

    def turn(v):
        v = v.astype(F32)
        return (v * cosine + pltpu.roll(v, HEAD_DIM // 2, 1) * sine).astype(BF16)

    key_all[me] = turn(k_ref[...])

    tri = jnp.where(row <= lane, 1.0, 0.0).astype(F32)
    cumul_t = dot(decay_ref[...], tri, precision=HIGHEST)
    pad_a[0:heads, :] = cumul_t
    pad_b[0:heads, :] = step_ref[...]
    cumul = jnp.transpose(pad_a[...])
    ending = cumul[TOKENS - 1 : TOKENS, :]
    ends_own[0] = ending
    ends_all[me] = ending
    carry_weight = jnp.transpose(pad_b[...]) * jnp.exp(ending - cumul)
    for load in loads[4:6]:
        load.wait()
    for j in range(pairs):
        weighted = x_ref[:, j * LANES : (j + 1) * LANES].astype(F32) * spread(carry_weight, j)
        turned = jnp.transpose(weighted).astype(BF16)
        local = dot(turned, write_ref[...]).astype(BF16)
        per = LANES // state_rows
        local_state[j * per : (j + 1) * per] = local.reshape(per, state_rows, LANES)
    state_in[me] = local_state[me]

    pl.semaphore_wait(barrier, ctx_size + exp_size - 2)

    def exchange(*moves):
        def one(i, c):
            peer = peer_of(i)
            for slot, source, target in moves:
                pltpu.make_async_remote_copy(
                    src_ref=source.at[peer if slot else 0],
                    dst_ref=target.at[me],
                    send_sem=a2a_send.at[slot],
                    recv_sem=a2a_recv.at[slot],
                    device_id={"ctx": peer},
                    device_id_type=MESH,
                ).start()
            return c

        lax.fori_loop(0, ctx_size - 1, one, 0, unroll=UNROLL)

    def exchange_wait(slot, target):
        whole = target.at[pl.ds(0, ctx_size - 1)]
        done = pltpu.make_async_remote_copy(
            src_ref=whole,
            dst_ref=whole,
            send_sem=a2a_send.at[slot],
            recv_sem=a2a_recv.at[slot],
            device_id={"ctx": me},
            device_id_type=MESH,
        )
        done.wait_send()
        done.wait_recv()

    key_length, value_length = half // SEGMENTS[0], half // SEGMENTS[1]
    block_b = jnp.where(my_y == 3, 1, 0)
    up_row = jnp.where(my_y == 1, 2, 3)
    right = my_y * z_size + lax.rem(my_z + 1, z_size)
    left = my_y * z_size + lax.rem(my_z + z_size - 1, z_size)

    def piece(buffer, recv, index, part):
        pieces = recv.shape[1]
        size = TOKENS // pieces
        at = index if pieces == 1 else (index, pl.ds(part * size, size))
        return buffer.at[at], recv.at[index, part]

    def push(buffer, recv, index, peer, sem, part=None):
        for p in range(recv.shape[1]) if part is None else (part,):
            block, landed = piece(buffer, recv, index, p)
            pltpu.make_async_remote_copy(
                src_ref=block,
                dst_ref=block,
                send_sem=sem,
                recv_sem=landed,
                device_id={"ctx": peer},
                device_id_type=MESH,
            ).start()

    def arrived(buffer, recv, index, sem, part=None):
        for p in range(recv.shape[1]) if part is None else (part,):
            block, landed = piece(buffer, recv, index, p)
            pltpu.make_async_remote_copy(
                src_ref=block,
                dst_ref=block,
                send_sem=sem,
                recv_sem=landed,
                device_id={"ctx": me},
                device_id_type=MESH,
            ).wait_recv()

    def at_distance(d):
        return lax.rem(my_z + d + 2 * z_size, z_size)

    def launch(buffer, recv, sem, length, row_y):
        for d in reversed(range(1, half + 1, length)):
            push(buffer, recv, me, row_y * z_size + at_distance(d), sem)
            if d < half:
                push(buffer, recv, me, row_y * z_size + at_distance(-d), sem)

    def lift(buffer, recv, index, sem, by_y, part=None):
        @pl.when(my_y < 3)
        def _():
            push(buffer, recv, index, up_row * z_size + my_z, sem, part)

        if by_y:

            @pl.when(my_y == 0)
            def _():
                push(buffer, recv, index, z_size + my_z, sem, part)

    def ring_open(buffer, recv, sem, length, by_y):
        launch(buffer, recv, sem, length, my_y)
        lift(buffer, recv, me, sem, by_y)
        if by_y:
            return

        @pl.when(my_y == 1)
        def _():
            launch(buffer, recv, sem, length, 3)
            push(buffer, recv, me, 3 * z_size + my_z, sem)

        @pl.when(my_y == 0)
        def _():
            launch(buffer, recv, sem, length, 2)
            launch(buffer, recv, sem, length, 1)
            push(buffer, recv, me, 2 * z_size + my_z, sem)
            push(buffer, recv, me, z_size + my_z, sem)

    def ring_steps(low, high, buffer, recv, sem, length, by_y, compute):
        segments = half // length

        def step(s, c):
            for source, lifted in ((my_y, True),) if by_y else ((my_y, True), (block_b, False)):
                if not lifted:

                    @pl.when((s == 0) & (my_y > 0))
                    def _():
                        index = block_b * z_size + my_z
                        arrived(buffer, recv, index, sem)

                for segment in range(segments):
                    for side in range(2):
                        hop = s - segment
                        d = hop + segment * length
                        ready = (hop >= 1) & (hop <= length) & (d <= half - side)
                        if not lifted:
                            ready = ready & (my_y > 0)

                        @pl.when(ready)
                        def _():
                            index = source * z_size + at_distance(d if side else -d)
                            for part in range(recv.shape[1]):
                                arrived(buffer, recv, index, sem, part)

                                @pl.when((hop < length) & (d < half - side))
                                def _():
                                    push(buffer, recv, index, left if side else right, sem, part)

                                if lifted:
                                    lift(buffer, recv, index, sem, by_y, part)

            def visit(j, c):
                segment, rest = lax.div(j, 2 * ROWS_Y), lax.rem(j, 2 * ROWS_Y)
                side, row_y = lax.div(rest, ROWS_Y), lax.rem(rest, ROWS_Y)
                if by_y:
                    relayed = row_y < my_y
                    twice = ((my_y == 2) & (row_y == 0)) | ((my_y == 3) & (row_y == 1))
                    lag = jnp.where(relayed, jnp.where(twice, 2, 1), 0)
                else:
                    relayed = (row_y != my_y) & (row_y != block_b) & (row_y < my_y)
                    lag = jnp.where(relayed, 1, 0)
                back = s - segment - lag
                d = back + segment * length
                index = row_y * z_size + at_distance(jnp.where(side == 0, -d, d))
                fits = (back <= length) & (d <= half - side)
                starts = (back >= 1) | ((back == 0) & (segment == 0) & (side == 0))
                valid = fits & starts & (row_y <= my_y)

                @pl.when(valid & relayed)
                def _():
                    arrived(buffer, recv, index, sem)

                if by_y:

                    @pl.when(valid & (my_y < 3) & (row_y + 1 == my_y))
                    def _():
                        push(buffer, recv, index, (my_y + 1) * z_size + my_z, sem)

                @pl.when(valid & (index < me))
                def _():
                    compute(index)

                return c

            lax.fori_loop(0, segments * 2 * ROWS_Y, visit, 0)
            return c

        lax.fori_loop(low, high, step, 0)

    def ring_last(length, by_y):
        return length + half // length + (2 if by_y else 1)

    def ring_close(buffer, sem, length, by_y):
        ring = z_size - 1
        opened = 2 * (half // length) - (1 if (half - 1) % length == 0 else 0)
        relays = ring - opened
        counts = (
            ring + z_size + 2 * (opened + 1),
            ring + z_size + opened + 1 + relays,
            ring + z_size + relays,
            ring + relays,
        )
        if by_y:
            counts = (ring + 2 * z_size,) * 3 + (ring,)
        for y, count in enumerate(counts):

            @pl.when(my_y == y)
            def _():
                for part in range(0, count, ctx_size):
                    size = min(ctx_size, count - part)
                    whole = buffer.at[pl.ds(0, size)]
                    pltpu.make_async_remote_copy(
                        src_ref=whole,
                        dst_ref=whole,
                        send_sem=sem,
                        recv_sem=sem,
                        device_id={"ctx": me},
                        device_id_type=MESH,
                    ).wait_send()

    ring_open(key_all, key_recv, ring_send.at[0], key_length, True)
    exchange((1, local_state, state_in), (0, ends_own, ends_all))
    for load in loads[6:]:
        load.wait()

    for g in range(groups):
        turned_q[g] = turn(q_ref[:, g * HEAD_DIM : (g + 1) * HEAD_DIM])

    def score(index):
        return dot(turned_q[...].reshape(groups * TOKENS, LANES), key_all[index], ((1,), (1,)))

    own_score = score(me)
    for g in range(groups):
        masked = jnp.where(causal, own_score[g * TOKENS : (g + 1) * TOKENS], LOWEST)
        score_ref[me, g] = masked
        top_ref[g] = masked

    def key_block(index):
        s = score(index).reshape(groups, TOKENS, LANES)
        score_ref[index] = s
        top_ref[...] = jnp.maximum(top_ref[...], s)

    gram = dot(read_ref[...], write_ref[...], ((1,), (1,)))
    for j in range(pairs):
        x_pair = x_ref[:, j * LANES : (j + 1) * LANES]
        total = None
        for part in range(2):
            h = 2 * j + part
            exponent = jnp.where(causal, cumul[:, h : h + 1] - cumul_t[h : h + 1, :], LOWEST)
            mixing = (jnp.exp(exponent) * gram * step_ref[h : h + 1, :]).astype(BF16)
            keep = first if part == 0 else jnp.logical_not(first)
            term = dot(mixing, jnp.where(keep, x_pair, jnp.zeros_like(x_pair)))
            total = term if total is None else total + term
        skip = jnp.where(
            first[0:1], skip_ref[0:1, 2 * j : 2 * j + 1], skip_ref[0:1, 2 * j + 1 : 2 * j + 2]
        )
        gated_ref[:, j * LANES : (j + 1) * LANES] = total + skip * x_pair.astype(F32)

    split_a, split_b = min(SPLIT[0], ring_last(key_length, True)), min(SPLIT[1], ring_last(key_length, True))
    ring_steps(0, split_a, key_all, key_recv, ring_send.at[0], key_length, True, key_block)

    exchange_wait(0, ends_all)
    head = lax.div(me * state_rows, MIXER_CHANNELS)
    chosen = jnp.where(row == head, 1.0, 0.0).astype(F32)
    decay_rows[...] = jnp.exp(
        dot(ends_all[...].reshape(ctx_size, LANES), chosen, precision=HIGHEST)
    )
    exchange_wait(1, state_in)

    def scan(b, state):
        state_out[b] = state.astype(BF16)
        return state * decay_rows[pl.ds(b, 1), :] + state_in[b].astype(F32)

    lax.fori_loop(0, ctx_size, scan, jnp.zeros((state_rows, LANES), F32), unroll=8)
    state_back[me] = state_out[me]
    exchange((2, state_out, state_back))

    ring_steps(split_a, split_b, key_all, key_recv, ring_send.at[0], key_length, True, key_block)

    exchange_wait(2, state_back)
    growth = jnp.exp(cumul)
    squares = jnp.zeros((TOKENS, LANES), F32)
    per = LANES // state_rows
    for j in range(pairs):
        at = slice(j * LANES, (j + 1) * LANES)
        state = state_back[j * per : (j + 1) * per].reshape(LANES, LANES)
        inter = dot(read_ref[...], state, ((1,), (1,))) * spread(growth, j)
        gate = gate_ref[:, at].astype(F32)
        gated = (gated_ref[:, at] + inter) * (gate / (1.0 + jnp.exp(-gate)))
        squares = squares + gated * gated
        scaled = gated * gain_ref[0:1, at]
        gated_ref[:, at] = scaled
        scaled_ref[:, at] = scaled.astype(BF16)
    ones = jnp.ones((8, LANES), F32)
    square_own[0] = dot(ones, squares, ((1,), (1,)), precision=HIGHEST)
    square_in[col] = square_own[0]

    def value_terms(e):
        at = pl.ds(pl.multiple_of(e * LANES, LANES), LANES)
        return dot(scaled_ref[...], weight_ref[:, at]).astype(BF16)

    def scatter(i, c):
        order = exp_size // 2 + (1 - 2 * lax.rem(i, 2)) * lax.div(i + 1, 2)
        peer = lax.rem(col + order, exp_size)
        pltpu.make_async_remote_copy(
            src_ref=square_own.at[0],
            dst_ref=square_in.at[col],
            send_sem=exp_send.at[0],
            recv_sem=exp_recv.at[0],
            device_id={"exp": peer},
            device_id_type=MESH,
        ).start()
        terms_ref[peer] = value_terms(peer)
        pltpu.make_async_remote_copy(
            src_ref=terms_ref.at[peer],
            dst_ref=terms_in.at[col],
            send_sem=exp_send.at[1],
            recv_sem=exp_recv.at[1],
            device_id={"exp": peer},
            device_id_type=MESH,
        ).start()
        return c

    lax.fori_loop(0, exp_size - 1, scatter, 0)
    terms_in[col] = value_terms(col)

    ring_steps(split_b, ring_last(key_length, True), key_all, key_recv, ring_send.at[0], key_length, True, key_block)
    ring_close(key_all, ring_send.at[0], key_length, True)

    for g in range(groups):
        top_ref[g] = jnp.broadcast_to(jnp.max(top_ref[g], axis=1, keepdims=True), (TOKENS, LANES))
        sum_ref[g] = jnp.zeros((TOKENS, LANES), F32)
        out_ref[g] = jnp.zeros((TOKENS, LANES), F32)

    def weigh(b, c):
        for g in range(groups):
            p = jnp.exp2((score_ref[b, g] - top_ref[g]) * EXP2_SCALE)
            sum_ref[g] += p
            prob_ref[b, g] = p.astype(BF16)
        return c

    lax.fori_loop(0, me + 1, weigh, 0)

    for slot, target in ((0, square_in), (1, terms_in)):
        whole = target.at[pl.ds(0, exp_size - 1)]
        done = pltpu.make_async_remote_copy(
            src_ref=whole,
            dst_ref=whole,
            send_sem=exp_send.at[slot],
            recv_sem=exp_recv.at[slot],
            device_id={"exp": col},
            device_id_type=MESH,
        )
        done.wait_send()
        done.wait_recv()
    square_row = square_in[0]
    for e in range(1, exp_size):
        square_row = square_row + square_in[e]
    square = jnp.transpose(jnp.broadcast_to(square_row[0:1, :], (TOKENS, LANES)))
    factor = lax.rsqrt(square * (1.0 / (exp_size * heads * MIXER_CHANNELS)) + NORM_EPS)
    value = terms_in[0].astype(F32)
    for e in range(1, exp_size):
        value = value + terms_in[e].astype(F32)
    value_all[me] = (value * factor).astype(BF16)
    ring_open(value_all, value_recv, ring_send.at[1], value_length, False)

    for j in range(pairs):
        at = slice(j * LANES, (j + 1) * LANES)
        mixer_ref[:, at] = (gated_ref[:, at] * factor).astype(BF16)

    def value_block(index):
        probs = prob_ref[index].reshape(groups * TOKENS, LANES)
        out_ref[...] += dot(probs, value_all[index]).reshape(groups, TOKENS, LANES)

    value_block(me)
    ring_steps(
        0, ring_last(value_length, False), value_all, value_recv, ring_send.at[1], value_length, False, value_block
    )
    for g in range(groups):
        total = jnp.sum(sum_ref[g], axis=1, keepdims=True)
        attn_ref[:, g * HEAD_DIM : (g + 1) * HEAD_DIM] = (out_ref[g] / total).astype(BF16)
    ring_close(value_all, ring_send.at[1], value_length, False)


def hand_over(attn_in, mixer_in, attn_out, mixer_out, sem):
    first = pltpu.make_async_copy(attn_in, attn_out, sem.at[0])
    second = pltpu.make_async_copy(mixer_in, mixer_out, sem.at[1])
    first.start()
    second.start()
    first.wait()
    second.wait()


SPLIT = (3, 8)
SEGMENTS = (1, 2)
PIECES = (1, 1)
INPUTS = 12
UNROLL = 7


def solution(mesh):
    ctx_size, exp_size = mesh.shape["ctx"], mesh.shape["exp"]

    def on_device(
        queries,
        key_rows,
        mixer_input,
        gate_input,
        write_proj,
        read_proj,
        step_size,
        log_decay,
        skip_gain,
        norm_gain,
        value_weight,
    ):
        heads = step_size.shape[1]
        channels = heads * MIXER_CHANNELS
        groups = queries.shape[1] // HEAD_DIM
        state_rows = channels // ctx_size
        frequency = ROPE_BASE ** (-(2.0 * np.arange(HEAD_DIM // 2)) / HEAD_DIM)
        frequency = jnp.asarray(np.tile(frequency, 2)[None, :], F32)
        tile = (TOKENS, LANES)
        anywhere = pl.BlockSpec(memory_space=pl.ANY)
        operands = (
            key_rows,
            log_decay.T,
            step_size.T,
            frequency,
            mixer_input,
            write_proj,
            read_proj,
            queries,
            skip_gain.reshape(1, heads),
            gate_input,
            norm_gain.reshape(1, channels),
            value_weight,
        )
        results = (
            jax.ShapeDtypeStruct(queries.shape, BF16),
            jax.ShapeDtypeStruct(mixer_input.shape, BF16),
        )
        staged = [pltpu.VMEM(a.shape, a.dtype) for a in operands]
        found = pl.pallas_call(
            functools.partial(kernel, ctx_size, exp_size),
            out_shape=tuple(pltpu.VMEM(a.shape, a.dtype) for a in results),
            in_specs=[anywhere] * INPUTS,
            out_specs=(pl.BlockSpec(memory_space=pltpu.VMEM),) * 2,
            scratch_shapes=staged
            + [
                pltpu.SemaphoreType.DMA((INPUTS,)),
                pltpu.VMEM((ctx_size, state_rows, LANES), BF16),
                pltpu.VMEM((ctx_size, state_rows, LANES), BF16),
                pltpu.VMEM((ctx_size, state_rows, LANES), BF16),
                pltpu.VMEM((ctx_size, state_rows, LANES), BF16),
                pltpu.VMEM((1, 1, LANES), F32),
                pltpu.VMEM((ctx_size, 1, LANES), F32),
                pltpu.VMEM(tile, F32),
                pltpu.VMEM(tile, F32),
                pltpu.VMEM((ctx_size, LANES), F32),
                pltpu.VMEM((TOKENS, channels), F32),
                pltpu.VMEM((TOKENS, channels), BF16),
                pltpu.VMEM((exp_size,) + tile, BF16),
                pltpu.VMEM((exp_size,) + tile, BF16),
                pltpu.VMEM((1, 8, LANES), F32),
                pltpu.VMEM((exp_size, 8, LANES), F32),
                pltpu.VMEM((groups,) + tile, BF16),
                pltpu.VMEM((ctx_size,) + tile, BF16),
                pltpu.VMEM((ctx_size,) + tile, BF16),
                pltpu.VMEM((ctx_size, groups) + tile, F32),
                pltpu.VMEM((ctx_size, groups) + tile, BF16),
                pltpu.VMEM((groups,) + tile, F32),
                pltpu.VMEM((groups,) + tile, F32),
                pltpu.VMEM((groups,) + tile, F32),
                pltpu.SemaphoreType.DMA((3,)),
                pltpu.SemaphoreType.DMA((3,)),
                pltpu.SemaphoreType.DMA((2,)),
                pltpu.SemaphoreType.DMA((2,)),
                pltpu.SemaphoreType.DMA((2,)),
                pltpu.SemaphoreType.DMA((ctx_size, PIECES[0])),
                pltpu.SemaphoreType.DMA((ctx_size, PIECES[1])),
            ],
            compiler_params=pltpu.CompilerParams(
                collective_id=0, has_side_effects=True, vmem_limit_bytes=56 * 1024 * 1024
            ),
        )(*operands)
        return pl.pallas_call(
            hand_over,
            out_shape=results,
            in_specs=[pl.BlockSpec(memory_space=pltpu.VMEM)] * 2,
            out_specs=(anywhere, anywhere),
            scratch_shapes=[pltpu.SemaphoreType.DMA((2,))],
            compiler_params=pltpu.CompilerParams(vmem_limit_bytes=2 * 1024 * 1024),
        )(*found)

    return jax.shard_map(
        on_device,
        mesh=mesh,
        in_specs=(
            P("ctx", "exp"),
            P("ctx", "exp"),
            P("ctx", "exp"),
            P("ctx", "exp"),
            P("ctx", None),
            P("ctx", None),
            P("ctx", "exp"),
            P("ctx", "exp"),
            P("exp"),
            P("exp"),
            P("exp", None),
        ),
        out_specs=(P("ctx", "exp"), P("ctx", "exp")),
        check_vma=False,
    )
```

```python
import functools

import jax
import jax.numpy as jnp
import numpy as np
from jax import lax
from jax.experimental import pallas as pl
from jax.experimental.pallas import tpu as pltpu
from jax.sharding import PartitionSpec as P

HEAD_DIM = 128
MIXER_CHANNELS = 64
TOKENS = 128
LANES = 128
ROWS_Y = 4
ROPE_BASE = 10000.0
ROPE_STRETCH = 4.0
NORM_EPS = 1e-05
LOWEST = -1e30
MESH = pl.DeviceIdType.MESH
F32 = jnp.float32
BF16 = jnp.bfloat16
HIGHEST = lax.Precision.HIGHEST
EXP2_SCALE = float(HEAD_DIM**-0.5 * np.log2(np.e))


def dot(a, b, dims=((1,), (0,)), precision=None):
    return lax.dot_general(
        a, b, (dims, ((), ())), precision=precision, preferred_element_type=F32
    )


def kernel(
    ctx_size,
    exp_size,
    *refs,
):
    inputs, refs = refs[:INPUTS], refs[INPUTS:]
    attn_ref, mixer_ref = refs[:2]
    staged, refs = refs[2 : 2 + INPUTS], refs[2 + INPUTS :]
    (
        k_ref,
        decay_ref,
        step_ref,
        freq_ref,
        x_ref,
        write_ref,
        read_ref,
        q_ref,
        skip_ref,
        gate_ref,
        gain_ref,
        weight_ref,
    ) = staged
    (
    load_sem,
    local_state,
    state_in,
    state_out,
    state_back,
    ends_own,
    ends_all,
    pad_a,
    pad_b,
    decay_rows,
    gated_ref,
    scaled_ref,
    terms_ref,
    terms_in,
    square_own,
    square_in,
    turned_q,
    key_all,
    value_all,
    score_ref,
    prob_ref,
    top_ref,
    sum_ref,
    out_ref,
    a2a_send,
    a2a_recv,
    exp_send,
    exp_recv,
    ring_send,
    key_recv,
    value_recv,
    ) = refs
    z_size = ctx_size // ROWS_Y
    half = z_size // 2
    heads = step_ref.shape[0]
    pairs = heads // 2
    groups = q_ref.shape[1] // HEAD_DIM
    state_rows = heads * MIXER_CHANNELS // ctx_size
    me = lax.axis_index("ctx")
    col = lax.axis_index("exp")
    my_y = lax.div(me, z_size)
    my_z = lax.rem(me, z_size)

    barrier = pltpu.get_barrier_semaphore()

    def peer_of(i):
        part, turn_y = lax.div(i, ROWS_Y), lax.rem(lax.rem(i, ROWS_Y) + 1, ROWS_Y)
        odd = lax.rem(part, 2)
        shift = half + (1 - 2 * odd) * lax.div(part + 1, 2)
        return lax.rem(my_y + turn_y, ROWS_Y) * z_size + lax.rem(my_z + shift, z_size)

    def greet_ctx(i, c):
        pl.semaphore_signal(
            barrier, inc=1, device_id={"ctx": peer_of(i)}, device_id_type=MESH
        )
        return c

    lax.fori_loop(0, ctx_size - 1, greet_ctx, 0, unroll=7 if ctx_size == 64 else 1)

    def greet_exp(i, c):
        pl.semaphore_signal(
            barrier, inc=1, device_id={"exp": lax.rem(col + i, exp_size)}, device_id_type=MESH
        )
        return c

    lax.fori_loop(1, exp_size, greet_exp, 0)
    loads = [
        pltpu.make_async_copy(a, b, load_sem.at[i]) for i, (a, b) in enumerate(zip(inputs, staged))
    ]
    for load in loads:
        load.start()
    pad_a[...] = jnp.zeros_like(pad_a)
    pad_b[...] = jnp.zeros_like(pad_b)
    for load in loads[:4]:
        load.wait()

    row = lax.broadcasted_iota(jnp.int32, (TOKENS, LANES), 0)
    lane = lax.broadcasted_iota(jnp.int32, (TOKENS, LANES), 1)
    first = lane < MIXER_CHANNELS
    causal = row >= lane

    def spread(columns, j):
        return jnp.where(first, columns[:, 2 * j : 2 * j + 1], columns[:, 2 * j + 1 : 2 * j + 2])

    position = (me * TOKENS + row).astype(F32)
    angle = (position * (1.0 / ROPE_STRETCH)) * freq_ref[...]
    cosine = jnp.cos(angle)
    sine = jnp.sin(angle)
    sine = jnp.where(first, -sine, sine)

    def turn(v):
        v = v.astype(F32)
        return (v * cosine + pltpu.roll(v, HEAD_DIM // 2, 1) * sine).astype(BF16)

    key_all[me] = turn(k_ref[...])

    tri = jnp.where(row <= lane, 1.0, 0.0).astype(F32)
    cumul_t = dot(decay_ref[...], tri, precision=HIGHEST)
    pad_a[0:heads, :] = cumul_t
    pad_b[0:heads, :] = step_ref[...]
    cumul = jnp.transpose(pad_a[...])
    ending = cumul[TOKENS - 1 : TOKENS, :]
    ends_own[0] = ending
    ends_all[me] = ending
    carry_weight = jnp.transpose(pad_b[...]) * jnp.exp(ending - cumul)
    for load in loads[4:6]:
        load.wait()
    for j in range(pairs):
        weighted = x_ref[:, j * LANES : (j + 1) * LANES].astype(F32) * spread(carry_weight, j)
        turned = jnp.transpose(weighted).astype(BF16)
        local = dot(turned, write_ref[...]).astype(BF16)
        per = LANES // state_rows
        local_state[j * per : (j + 1) * per] = local.reshape(per, state_rows, LANES)
    state_in[me] = local_state[me]

    pl.semaphore_wait(barrier, ctx_size + exp_size - 2)

    def exchange(low, high, *moves):
        def one(i, c):
            peer = peer_of(i)
            for slot, source, target in moves:
                pltpu.make_async_remote_copy(
                    src_ref=source.at[peer if slot else 0],
                    dst_ref=target.at[me],
                    send_sem=a2a_send.at[slot],
                    recv_sem=a2a_recv.at[slot],
                    device_id={"ctx": peer},
                    device_id_type=MESH,
                ).start()
            return c

        lax.fori_loop(low, high, one, 0, unroll=4 if (high - low) % 4 == 0 else 5 if (high - low) % 5 == 0 else 1)

    def exchange_wait(slot, target, sent=False):
        whole = target.at[pl.ds(0, ctx_size - 1)]
        done = pltpu.make_async_remote_copy(
            src_ref=whole,
            dst_ref=whole,
            send_sem=a2a_send.at[slot],
            recv_sem=a2a_recv.at[slot],
            device_id={"ctx": me},
            device_id_type=MESH,
        )
        done.wait_send() if sent else done.wait_recv()

    key_length, value_length = half // SEGMENTS[0], half // SEGMENTS[1]
    block_b = jnp.where(my_y == 3, 1, 0)
    up_row = jnp.where(my_y == 1, 2, 3)
    right = my_y * z_size + lax.rem(my_z + 1, z_size)
    left = my_y * z_size + lax.rem(my_z + z_size - 1, z_size)

    def piece(buffer, recv, index, part):
        pieces = recv.shape[1]
        size = TOKENS // pieces
        at = index if pieces == 1 else (index, pl.ds(part * size, size))
        return buffer.at[at], recv.at[index, part]

    def push(buffer, recv, index, peer, sem, part=None):
        for p in range(recv.shape[1]) if part is None else (part,):
            block, landed = piece(buffer, recv, index, p)
            pltpu.make_async_remote_copy(
                src_ref=block,
                dst_ref=block,
                send_sem=sem,
                recv_sem=landed,
                device_id={"ctx": peer},
                device_id_type=MESH,
            ).start()

    def arrived(buffer, recv, index, sem, part=None):
        for p in range(recv.shape[1]) if part is None else (part,):
            block, landed = piece(buffer, recv, index, p)
            pltpu.make_async_remote_copy(
                src_ref=block,
                dst_ref=block,
                send_sem=sem,
                recv_sem=landed,
                device_id={"ctx": me},
                device_id_type=MESH,
            ).wait_recv()

    def at_distance(d):
        return lax.rem(my_z + d + 2 * z_size, z_size)

    def launch(buffer, recv, sem, length, row_y):
        for d in reversed(range(1, half + 1, length)):
            push(buffer, recv, me, row_y * z_size + at_distance(d), sem)
            if d < half:
                push(buffer, recv, me, row_y * z_size + at_distance(-d), sem)

    def lift(buffer, recv, index, sem, by_y, part=None):
        @pl.when(my_y < 3)
        def _():
            push(buffer, recv, index, up_row * z_size + my_z, sem, part)

        if by_y:

            @pl.when(my_y == 0)
            def _():
                push(buffer, recv, index, z_size + my_z, sem, part)

    def ring_open(buffer, recv, sem, length, by_y):
        launch(buffer, recv, sem, length, my_y)
        lift(buffer, recv, me, sem, by_y)
        if by_y:
            return

        @pl.when(my_y == 1)
        def _():
            launch(buffer, recv, sem, length, 3)
            push(buffer, recv, me, 3 * z_size + my_z, sem)

        @pl.when(my_y == 0)
        def _():
            launch(buffer, recv, sem, length, 2)
            launch(buffer, recv, sem, length, 1)
            push(buffer, recv, me, 2 * z_size + my_z, sem)
            push(buffer, recv, me, z_size + my_z, sem)

    def ring_steps(low, high, buffer, recv, sem, length, by_y, compute):
        segments = half // length

        def step(s, c):
            for source, lifted in ((my_y, True),) if by_y else ((my_y, True), (block_b, False)):
                if not lifted:

                    @pl.when((s == 0) & (my_y > 0))
                    def _():
                        index = block_b * z_size + my_z
                        arrived(buffer, recv, index, sem)

                for segment in range(segments):
                    for side in range(2):
                        hop = s - segment
                        d = hop + segment * length
                        ready = (hop >= 1) & (hop <= length) & (d <= half - side)
                        if not lifted:
                            ready = ready & (my_y > 0)

                        @pl.when(ready)
                        def _():
                            index = source * z_size + at_distance(d if side else -d)
                            for part in range(recv.shape[1]):
                                arrived(buffer, recv, index, sem, part)

                                @pl.when((hop < length) & (d < half - side))
                                def _():
                                    push(buffer, recv, index, left if side else right, sem, part)

                                if lifted:
                                    lift(buffer, recv, index, sem, by_y, part)

            def visit(j, c):
                segment, rest = lax.div(j, 2 * ROWS_Y), lax.rem(j, 2 * ROWS_Y)
                side, row_y = lax.div(rest, ROWS_Y), lax.rem(rest, ROWS_Y)
                if by_y:
                    relayed = row_y < my_y
                    twice = ((my_y == 2) & (row_y == 0)) | ((my_y == 3) & (row_y == 1))
                    lag = jnp.where(relayed, jnp.where(twice, 2, 1), 0)
                else:
                    relayed = (row_y != my_y) & (row_y != block_b) & (row_y < my_y)
                    lag = jnp.where(relayed, 1, 0)
                back = s - segment - lag
                d = back + segment * length
                index = row_y * z_size + at_distance(jnp.where(side == 0, -d, d))
                fits = (back <= length) & (d <= half - side)
                starts = (back >= 1) | ((back == 0) & (segment == 0) & (side == 0))
                valid = fits & starts & (row_y <= my_y)

                @pl.when(valid & relayed)
                def _():
                    arrived(buffer, recv, index, sem)

                if by_y:

                    @pl.when(valid & (my_y < 3) & (row_y + 1 == my_y))
                    def _():
                        push(buffer, recv, index, (my_y + 1) * z_size + my_z, sem)

                @pl.when(valid & (index < me))
                def _():
                    compute(index)

                return c

            lax.fori_loop(0, segments * 2 * ROWS_Y, visit, 0)
            return c

        lax.fori_loop(low, high, step, 0)

    def ring_last(length, by_y):
        return length + half // length + (2 if by_y else 1)

    def ring_close(buffer, sem, length, by_y):
        ring = z_size - 1
        opened = 2 * (half // length) - (1 if (half - 1) % length == 0 else 0)
        relays = ring - opened
        counts = (
            ring + z_size + 2 * (opened + 1),
            ring + z_size + opened + 1 + relays,
            ring + z_size + relays,
            ring + relays,
        )
        if by_y:
            counts = (ring + 2 * z_size,) * 3 + (ring,)
        for y, count in enumerate(counts):

            @pl.when(my_y == y)
            def _():
                for part in range(0, count, ctx_size):
                    size = min(ctx_size, count - part)
                    whole = buffer.at[pl.ds(0, size)]
                    pltpu.make_async_remote_copy(
                        src_ref=whole,
                        dst_ref=whole,
                        send_sem=sem,
                        recv_sem=sem,
                        device_id={"ctx": me},
                        device_id_type=MESH,
                    ).wait_send()

    ring_open(key_all, key_recv, ring_send.at[0], key_length, True)
    cuts = [ctx_size * part // SHARES for part in range(SHARES)] + [ctx_size - 1]
    outgoing = ((1, local_state, state_in), (0, ends_own, ends_all))
    exchange(cuts[0], cuts[1], *outgoing)
    for load in loads[6:]:
        load.wait()

    for g in range(groups):
        turned_q[g] = turn(q_ref[:, g * HEAD_DIM : (g + 1) * HEAD_DIM])

    def score(index):
        return dot(turned_q[...].reshape(groups * TOKENS, LANES), key_all[index], ((1,), (1,)))

    own_score = score(me)
    for g in range(groups):
        masked = jnp.where(causal, own_score[g * TOKENS : (g + 1) * TOKENS], LOWEST)
        score_ref[me, g] = masked
        top_ref[g] = masked

    def key_block(index):
        s = score(index).reshape(groups, TOKENS, LANES)
        score_ref[index] = s
        top_ref[...] = jnp.maximum(top_ref[...], s)

    gram = dot(read_ref[...], write_ref[...], ((1,), (1,)))
    for j in range(pairs):
        x_pair = x_ref[:, j * LANES : (j + 1) * LANES]
        total = None
        for part in range(2):
            h = 2 * j + part
            exponent = jnp.where(causal, cumul[:, h : h + 1] - cumul_t[h : h + 1, :], LOWEST)
            mixing = (jnp.exp(exponent) * gram * step_ref[h : h + 1, :]).astype(BF16)
            keep = first if part == 0 else jnp.logical_not(first)
            term = dot(mixing, jnp.where(keep, x_pair, jnp.zeros_like(x_pair)))
            total = term if total is None else total + term
        skip = jnp.where(
            first[0:1], skip_ref[0:1, 2 * j : 2 * j + 1], skip_ref[0:1, 2 * j + 1 : 2 * j + 2]
        )
        gated_ref[:, j * LANES : (j + 1) * LANES] = total + skip * x_pair.astype(F32)

    total_steps = ring_last(key_length, True)
    done = [0]

    def key_steps(upto):
        upto = min(upto, total_steps)
        if upto > done[0]:
            ring_steps(
                done[0], upto, key_all, key_recv, ring_send.at[0], key_length, True, key_block
            )
        done[0] = max(upto, done[0])

    for part in range(1, SHARES):
        key_steps(STEPS[0][part - 1])
        exchange(cuts[part], cuts[part + 1], *outgoing)
    key_steps(STEPS[0][SHARES - 1])

    exchange_wait(0, ends_all)
    head = lax.div(me * state_rows, MIXER_CHANNELS)
    chosen = jnp.where(row == head, 1.0, 0.0).astype(F32)
    decay_rows[...] = jnp.exp(
        dot(ends_all[...].reshape(ctx_size, LANES), chosen, precision=HIGHEST)
    )
    exchange_wait(1, state_in)

    def scan(b, state):
        state_out[b] = state.astype(BF16)
        return state * decay_rows[pl.ds(b, 1), :] + state_in[b].astype(F32)

    lax.fori_loop(0, ctx_size, scan, jnp.zeros((state_rows, LANES), F32), unroll=8)
    state_back[me] = state_out[me]
    for part in range(SHARES):
        exchange(cuts[part], cuts[part + 1], (2, state_out, state_back))
        key_steps(STEPS[1][part])


    exchange_wait(2, state_back)
    growth = jnp.exp(cumul)
    squares = jnp.zeros((TOKENS, LANES), F32)
    per = LANES // state_rows
    for j in range(pairs):
        at = slice(j * LANES, (j + 1) * LANES)
        state = state_back[j * per : (j + 1) * per].reshape(LANES, LANES)
        inter = dot(read_ref[...], state, ((1,), (1,))) * spread(growth, j)
        gate = gate_ref[:, at].astype(F32)
        gated = (gated_ref[:, at] + inter) * (gate / (1.0 + jnp.exp(-gate)))
        squares = squares + gated * gated
        scaled = gated * gain_ref[0:1, at]
        gated_ref[:, at] = scaled
        scaled_ref[:, at] = scaled.astype(BF16)
    ones = jnp.ones((8, LANES), F32)
    square_own[0] = dot(ones, squares, ((1,), (1,)), precision=HIGHEST)
    square_in[col] = square_own[0]

    def value_terms(e):
        at = pl.ds(pl.multiple_of(e * LANES, LANES), LANES)
        return dot(scaled_ref[...], weight_ref[:, at]).astype(BF16)

    def scatter(i, c):
        order = exp_size // 2 + (1 - 2 * lax.rem(i, 2)) * lax.div(i + 1, 2)
        peer = lax.rem(col + order, exp_size)
        pltpu.make_async_remote_copy(
            src_ref=square_own.at[0],
            dst_ref=square_in.at[col],
            send_sem=exp_send.at[0],
            recv_sem=exp_recv.at[0],
            device_id={"exp": peer},
            device_id_type=MESH,
        ).start()
        terms_ref[peer] = value_terms(peer)
        pltpu.make_async_remote_copy(
            src_ref=terms_ref.at[peer],
            dst_ref=terms_in.at[col],
            send_sem=exp_send.at[1],
            recv_sem=exp_recv.at[1],
            device_id={"exp": peer},
            device_id_type=MESH,
        ).start()
        return c

    lax.fori_loop(0, exp_size - 1, scatter, 0)
    terms_in[col] = value_terms(col)

    key_steps(total_steps)

    for g in range(groups):
        top_ref[g] = jnp.broadcast_to(jnp.max(top_ref[g], axis=1, keepdims=True), (TOKENS, LANES))
        sum_ref[g] = jnp.zeros((TOKENS, LANES), F32)
        out_ref[g] = jnp.zeros((TOKENS, LANES), F32)

    def weigh(b, c):
        for g in range(groups):
            p = jnp.exp2((score_ref[b, g] - top_ref[g]) * EXP2_SCALE)
            sum_ref[g] += p
            prob_ref[b, g] = p.astype(BF16)
        return c

    lax.fori_loop(0, me + 1, weigh, 0)

    def scatter_wait(slot, target, sent=False):
        whole = target.at[pl.ds(0, exp_size - 1)]
        done = pltpu.make_async_remote_copy(
            src_ref=whole,
            dst_ref=whole,
            send_sem=exp_send.at[slot],
            recv_sem=exp_recv.at[slot],
            device_id={"exp": col},
            device_id_type=MESH,
        )
        done.wait_send() if sent else done.wait_recv()

    for slot, target in ((0, square_in), (1, terms_in)):
        scatter_wait(slot, target)
    square_row = square_in[0]
    for e in range(1, exp_size):
        square_row = square_row + square_in[e]
    square = jnp.transpose(jnp.broadcast_to(square_row[0:1, :], (TOKENS, LANES)))
    factor = lax.rsqrt(square * (1.0 / (exp_size * heads * MIXER_CHANNELS)) + NORM_EPS)
    value = terms_in[0].astype(F32)
    for e in range(1, exp_size):
        value = value + terms_in[e].astype(F32)
    value_all[me] = (value * factor).astype(BF16)
    ring_open(value_all, value_recv, ring_send.at[1], value_length, False)

    for j in range(pairs):
        at = slice(j * LANES, (j + 1) * LANES)
        mixer_ref[:, at] = (gated_ref[:, at] * factor).astype(BF16)

    def value_block(index):
        probs = prob_ref[index].reshape(groups * TOKENS, LANES)
        out_ref[...] += dot(probs, value_all[index]).reshape(groups, TOKENS, LANES)

    value_block(me)
    ring_steps(
        0, ring_last(value_length, False), value_all, value_recv, ring_send.at[1], value_length, False, value_block
    )
    for g in range(groups):
        total = jnp.sum(sum_ref[g], axis=1, keepdims=True)
        attn_ref[:, g * HEAD_DIM : (g + 1) * HEAD_DIM] = (out_ref[g] / total).astype(BF16)
    ring_close(key_all, ring_send.at[0], key_length, True)
    ring_close(value_all, ring_send.at[1], value_length, False)
    for slot, target in ((0, ends_all), (1, state_in), (2, state_back)):
        exchange_wait(slot, target, True)
    for slot, target in ((0, square_in), (1, terms_in)):
        scatter_wait(slot, target, True)


def hand_over(attn_in, mixer_in, attn_out, mixer_out, sem):
    first = pltpu.make_async_copy(attn_in, attn_out, sem.at[0])
    second = pltpu.make_async_copy(mixer_in, mixer_out, sem.at[1])
    first.start()
    second.start()
    first.wait()
    second.wait()


SHARES = 2
STEPS = ((2, 4), (6, 8))
SEGMENTS = (1, 2)
PIECES = (1, 1)
INPUTS = 12


def solution(mesh):
    ctx_size, exp_size = mesh.shape["ctx"], mesh.shape["exp"]

    def on_device(
        queries,
        key_rows,
        mixer_input,
        gate_input,
        write_proj,
        read_proj,
        step_size,
        log_decay,
        skip_gain,
        norm_gain,
        value_weight,
    ):
        heads = step_size.shape[1]
        channels = heads * MIXER_CHANNELS
        groups = queries.shape[1] // HEAD_DIM
        state_rows = channels // ctx_size
        frequency = ROPE_BASE ** (-(2.0 * np.arange(HEAD_DIM // 2)) / HEAD_DIM)
        frequency = jnp.asarray(np.tile(frequency, 2)[None, :], F32)
        tile = (TOKENS, LANES)
        anywhere = pl.BlockSpec(memory_space=pl.ANY)
        operands = (
            key_rows,
            log_decay.T,
            step_size.T,
            frequency,
            mixer_input,
            write_proj,
            read_proj,
            queries,
            skip_gain.reshape(1, heads),
            gate_input,
            norm_gain.reshape(1, channels),
            value_weight,
        )
        results = (
            jax.ShapeDtypeStruct(queries.shape, BF16),
            jax.ShapeDtypeStruct(mixer_input.shape, BF16),
        )
        staged = [pltpu.VMEM(a.shape, a.dtype) for a in operands]
        found = pl.pallas_call(
            functools.partial(kernel, ctx_size, exp_size),
            out_shape=tuple(pltpu.VMEM(a.shape, a.dtype) for a in results),
            in_specs=[anywhere] * INPUTS,
            out_specs=(pl.BlockSpec(memory_space=pltpu.VMEM),) * 2,
            scratch_shapes=staged
            + [
                pltpu.SemaphoreType.DMA((INPUTS,)),
                pltpu.VMEM((ctx_size, state_rows, LANES), BF16),
                pltpu.VMEM((ctx_size, state_rows, LANES), BF16),
                pltpu.VMEM((ctx_size, state_rows, LANES), BF16),
                pltpu.VMEM((ctx_size, state_rows, LANES), BF16),
                pltpu.VMEM((1, 1, LANES), F32),
                pltpu.VMEM((ctx_size, 1, LANES), F32),
                pltpu.VMEM(tile, F32),
                pltpu.VMEM(tile, F32),
                pltpu.VMEM((ctx_size, LANES), F32),
                pltpu.VMEM((TOKENS, channels), F32),
                pltpu.VMEM((TOKENS, channels), BF16),
                pltpu.VMEM((exp_size,) + tile, BF16),
                pltpu.VMEM((exp_size,) + tile, BF16),
                pltpu.VMEM((1, 8, LANES), F32),
                pltpu.VMEM((exp_size, 8, LANES), F32),
                pltpu.VMEM((groups,) + tile, BF16),
                pltpu.VMEM((ctx_size,) + tile, BF16),
                pltpu.VMEM((ctx_size,) + tile, BF16),
                pltpu.VMEM((ctx_size, groups) + tile, F32),
                pltpu.VMEM((ctx_size, groups) + tile, BF16),
                pltpu.VMEM((groups,) + tile, F32),
                pltpu.VMEM((groups,) + tile, F32),
                pltpu.VMEM((groups,) + tile, F32),
                pltpu.SemaphoreType.DMA((3,)),
                pltpu.SemaphoreType.DMA((3,)),
                pltpu.SemaphoreType.DMA((2,)),
                pltpu.SemaphoreType.DMA((2,)),
                pltpu.SemaphoreType.DMA((2,)),
                pltpu.SemaphoreType.DMA((ctx_size, PIECES[0])),
                pltpu.SemaphoreType.DMA((ctx_size, PIECES[1])),
            ],
            compiler_params=pltpu.CompilerParams(
                collective_id=0, has_side_effects=True, vmem_limit_bytes=56 * 1024 * 1024
            ),
        )(*operands)
        return pl.pallas_call(
            hand_over,
            out_shape=results,
            in_specs=[pl.BlockSpec(memory_space=pltpu.VMEM)] * 2,
            out_specs=(anywhere, anywhere),
            scratch_shapes=[pltpu.SemaphoreType.DMA((2,))],
            compiler_params=pltpu.CompilerParams(vmem_limit_bytes=2 * 1024 * 1024),
        )(*found)

    return jax.shard_map(
        on_device,
        mesh=mesh,
        in_specs=(
            P("ctx", "exp"),
            P("ctx", "exp"),
            P("ctx", "exp"),
            P("ctx", "exp"),
            P("ctx", None),
            P("ctx", None),
            P("ctx", "exp"),
            P("ctx", "exp"),
            P("exp"),
            P("exp"),
            P("exp", None),
        ),
        out_specs=(P("ctx", "exp"), P("ctx", "exp")),
        check_vma=False,
    )
```

```python
import functools

import jax
import jax.numpy as jnp
import numpy as np
from jax import lax
from jax.experimental import pallas as pl
from jax.experimental.pallas import tpu as pltpu
from jax.sharding import PartitionSpec as P

HEAD_DIM = 128
MIXER_CHANNELS = 64
TOKENS = 128
LANES = 128
ROWS_Y = 4
ROPE_BASE = 10000.0
ROPE_STRETCH = 4.0
NORM_EPS = 1e-05
LOWEST = -1e30
MESH = pl.DeviceIdType.MESH
F32 = jnp.float32
BF16 = jnp.bfloat16
HIGHEST = lax.Precision.HIGHEST
EXP2_SCALE = float(HEAD_DIM**-0.5 * np.log2(np.e))


def dot(a, b, dims=((1,), (0,)), precision=None):
    return lax.dot_general(
        a, b, (dims, ((), ())), precision=precision, preferred_element_type=F32
    )


def kernel(
    ctx_size,
    exp_size,
    *refs,
):
    inputs, refs = refs[:INPUTS], refs[INPUTS:]
    attn_ref, mixer_ref = refs[:2]
    staged, refs = refs[2 : 2 + INPUTS], refs[2 + INPUTS :]
    (
        k_ref,
        decay_ref,
        step_ref,
        freq_ref,
        x_ref,
        write_ref,
        read_ref,
        q_ref,
        skip_ref,
        gate_ref,
        gain_ref,
        weight_ref,
    ) = staged
    (
    load_sem,
    local_state,
    state_in,
    state_out,
    state_back,
    ends_own,
    ends_all,
    pad_a,
    pad_b,
    decay_rows,
    gated_ref,
    scaled_ref,
    terms_ref,
    terms_in,
    square_own,
    square_in,
    turned_q,
    key_all,
    value_all,
    score_ref,
    prob_ref,
    top_ref,
    sum_ref,
    out_ref,
    a2a_send,
    a2a_recv,
    exp_send,
    exp_recv,
    ring_send,
    key_recv,
    value_recv,
    ) = refs
    z_size = ctx_size // ROWS_Y
    half = z_size // 2
    heads = step_ref.shape[0]
    pairs = heads // 2
    groups = q_ref.shape[1] // HEAD_DIM
    state_rows = heads * MIXER_CHANNELS // ctx_size
    me = lax.axis_index("ctx")
    col = lax.axis_index("exp")
    my_y = lax.div(me, z_size)
    my_z = lax.rem(me, z_size)

    barrier = pltpu.get_barrier_semaphore()

    def peer_of(i):
        part, turn_y = lax.div(i, ROWS_Y), lax.rem(lax.rem(i, ROWS_Y) + 1, ROWS_Y)
        odd = lax.rem(part, 2)
        shift = half + (1 - 2 * odd) * lax.div(part + 1, 2)
        return lax.rem(my_y + turn_y, ROWS_Y) * z_size + lax.rem(my_z + shift, z_size)

    def greet_ctx(i, c):
        pl.semaphore_signal(
            barrier, inc=1, device_id={"ctx": peer_of(i)}, device_id_type=MESH
        )
        return c

    lax.fori_loop(0, ctx_size - 1, greet_ctx, 0, unroll=7 if ctx_size == 64 else 1)

    def greet_exp(i, c):
        pl.semaphore_signal(
            barrier, inc=1, device_id={"exp": lax.rem(col + i, exp_size)}, device_id_type=MESH
        )
        return c

    lax.fori_loop(1, exp_size, greet_exp, 0)
    loads = [
        pltpu.make_async_copy(a, b, load_sem.at[i]) for i, (a, b) in enumerate(zip(inputs, staged))
    ]
    for load in loads:
        load.start()
    pad_a[...] = jnp.zeros_like(pad_a)
    pad_b[...] = jnp.zeros_like(pad_b)
    for load in loads[:4]:
        load.wait()

    row = lax.broadcasted_iota(jnp.int32, (TOKENS, LANES), 0)
    lane = lax.broadcasted_iota(jnp.int32, (TOKENS, LANES), 1)
    first = lane < MIXER_CHANNELS
    causal = row >= lane

    def spread(columns, j):
        return jnp.where(first, columns[:, 2 * j : 2 * j + 1], columns[:, 2 * j + 1 : 2 * j + 2])

    position = (me * TOKENS + row).astype(F32)
    angle = (position * (1.0 / ROPE_STRETCH)) * freq_ref[...]
    cosine = jnp.cos(angle)
    sine = jnp.sin(angle)
    sine = jnp.where(first, -sine, sine)

    def turn(v):
        v = v.astype(F32)
        return (v * cosine + pltpu.roll(v, HEAD_DIM // 2, 1) * sine).astype(BF16)

    key_all[me] = turn(k_ref[...])

    tri = jnp.where(row <= lane, 1.0, 0.0).astype(F32)
    cumul_t = dot(decay_ref[...], tri, precision=HIGHEST)
    pad_a[0:heads, :] = cumul_t
    pad_b[0:heads, :] = step_ref[...]
    cumul = jnp.transpose(pad_a[...])
    ending = cumul[TOKENS - 1 : TOKENS, :]
    ends_own[0] = ending
    ends_all[me] = ending
    carry_weight = jnp.transpose(pad_b[...]) * jnp.exp(ending - cumul)
    for load in loads[4:6]:
        load.wait()
    for j in range(pairs):
        weighted = x_ref[:, j * LANES : (j + 1) * LANES].astype(F32) * spread(carry_weight, j)
        turned = jnp.transpose(weighted).astype(BF16)
        local = dot(turned, write_ref[...]).astype(BF16)
        per = LANES // state_rows
        local_state[j * per : (j + 1) * per] = local.reshape(per, state_rows, LANES)
    state_in[me] = local_state[me]

    pl.semaphore_wait(barrier, ctx_size + exp_size - 2)

    def exchange(low, high, *moves):
        def one(i, c):
            peer = peer_of(i)
            for slot, source, target in moves:
                pltpu.make_async_remote_copy(
                    src_ref=source.at[peer if slot else 0],
                    dst_ref=target.at[me],
                    send_sem=a2a_send.at[slot],
                    recv_sem=a2a_recv.at[slot],
                    device_id={"ctx": peer},
                    device_id_type=MESH,
                ).start()
            return c

        lax.fori_loop(low, high, one, 0, unroll=4 if (high - low) % 4 == 0 else 5 if (high - low) % 5 == 0 else 1)

    def exchange_wait(slot, target, sent=False):
        whole = target.at[pl.ds(0, ctx_size - 1)]
        done = pltpu.make_async_remote_copy(
            src_ref=whole,
            dst_ref=whole,
            send_sem=a2a_send.at[slot],
            recv_sem=a2a_recv.at[slot],
            device_id={"ctx": me},
            device_id_type=MESH,
        )
        done.wait_send() if sent else done.wait_recv()

    key_length, value_length = half // SEGMENTS[0], half // SEGMENTS[1]
    block_b = jnp.where(my_y == 3, 1, 0)
    up_row = jnp.where(my_y == 1, 2, 3)
    right = my_y * z_size + lax.rem(my_z + 1, z_size)
    left = my_y * z_size + lax.rem(my_z + z_size - 1, z_size)

    def piece(buffer, recv, index, part):
        pieces = recv.shape[1]
        size = TOKENS // pieces
        at = index if pieces == 1 else (index, pl.ds(part * size, size))
        return buffer.at[at], recv.at[index, part]

    def push(buffer, recv, index, peer, sem, part=None):
        for p in range(recv.shape[1]) if part is None else (part,):
            block, landed = piece(buffer, recv, index, p)
            pltpu.make_async_remote_copy(
                src_ref=block,
                dst_ref=block,
                send_sem=sem,
                recv_sem=landed,
                device_id={"ctx": peer},
                device_id_type=MESH,
            ).start()

    def arrived(buffer, recv, index, sem, part=None):
        for p in range(recv.shape[1]) if part is None else (part,):
            block, landed = piece(buffer, recv, index, p)
            pltpu.make_async_remote_copy(
                src_ref=block,
                dst_ref=block,
                send_sem=sem,
                recv_sem=landed,
                device_id={"ctx": me},
                device_id_type=MESH,
            ).wait_recv()

    def at_distance(d):
        return lax.rem(my_z + d + 2 * z_size, z_size)

    def launch(buffer, recv, sem, length, row_y):
        for d in reversed(range(1, half + 1, length)):
            push(buffer, recv, me, row_y * z_size + at_distance(d), sem)
            if d < half:
                push(buffer, recv, me, row_y * z_size + at_distance(-d), sem)

    def lift(buffer, recv, index, sem, by_y, part=None):
        @pl.when(my_y < 3)
        def _():
            push(buffer, recv, index, up_row * z_size + my_z, sem, part)

        if by_y:

            @pl.when(my_y == 0)
            def _():
                push(buffer, recv, index, z_size + my_z, sem, part)

    def ring_open(buffer, recv, sem, length, by_y):
        launch(buffer, recv, sem, length, my_y)
        lift(buffer, recv, me, sem, by_y)
        if by_y:
            return

        @pl.when(my_y == 1)
        def _():
            launch(buffer, recv, sem, length, 3)
            push(buffer, recv, me, 3 * z_size + my_z, sem)

        @pl.when(my_y == 0)
        def _():
            launch(buffer, recv, sem, length, 2)
            launch(buffer, recv, sem, length, 1)
            push(buffer, recv, me, 2 * z_size + my_z, sem)
            push(buffer, recv, me, z_size + my_z, sem)

    def ring_steps(low, high, buffer, recv, sem, length, by_y, compute):
        segments = half // length

        def step(s, c):
            for source, lifted in ((my_y, True),) if by_y else ((my_y, True), (block_b, False)):
                if not lifted:

                    @pl.when((s == 0) & (my_y > 0))
                    def _():
                        index = block_b * z_size + my_z
                        arrived(buffer, recv, index, sem)

                for segment in range(segments):
                    for side in range(2):
                        hop = s
                        d = hop + segment * length
                        ready = (hop >= 1) & (hop <= length) & (d <= half - side)
                        if not lifted:
                            ready = ready & (my_y > 0)

                        @pl.when(ready)
                        def _():
                            index = source * z_size + at_distance(d if side else -d)
                            for part in range(recv.shape[1]):
                                arrived(buffer, recv, index, sem, part)

                                @pl.when((hop < length) & (d < half - side))
                                def _():
                                    push(buffer, recv, index, left if side else right, sem, part)

                                if lifted:
                                    lift(buffer, recv, index, sem, by_y, part)

            def visit(j, c):
                segment, rest = lax.div(j, 2 * ROWS_Y), lax.rem(j, 2 * ROWS_Y)
                side, row_y = lax.div(rest, ROWS_Y), lax.rem(rest, ROWS_Y)
                if by_y:
                    relayed = row_y < my_y
                    twice = ((my_y == 2) & (row_y == 0)) | ((my_y == 3) & (row_y == 1))
                    lag = jnp.where(relayed, jnp.where(twice, 2, 1), 0)
                else:
                    relayed = (row_y != my_y) & (row_y != block_b) & (row_y < my_y)
                    lag = jnp.where(relayed, 1, 0)
                back = s - lag
                d = back + segment * length
                index = row_y * z_size + at_distance(jnp.where(side == 0, -d, d))
                fits = (back <= length) & (d <= half - side)
                starts = (back >= 1) | ((back == 0) & (segment == 0) & (side == 0))
                valid = fits & starts & (row_y <= my_y)

                @pl.when(valid & relayed)
                def _():
                    arrived(buffer, recv, index, sem)

                if by_y:

                    @pl.when(valid & (my_y < 3) & (row_y + 1 == my_y))
                    def _():
                        push(buffer, recv, index, (my_y + 1) * z_size + my_z, sem)

                @pl.when(valid & (index < me))
                def _():
                    compute(index)

                return c

            lax.fori_loop(0, segments * 2 * ROWS_Y, visit, 0)
            return c

        lax.fori_loop(low, high, step, 0)

    def ring_last(length, by_y):
        return length + (3 if by_y else 2)

    def ring_close(buffer, sem, length, by_y):
        ring = z_size - 1
        opened = 2 * (half // length) - (1 if (half - 1) % length == 0 else 0)
        relays = ring - opened
        counts = (
            ring + z_size + 2 * (opened + 1),
            ring + z_size + opened + 1 + relays,
            ring + z_size + relays,
            ring + relays,
        )
        if by_y:
            counts = (ring + 2 * z_size,) * 3 + (ring,)
        for y, count in enumerate(counts):

            @pl.when(my_y == y)
            def _():
                for part in range(0, count, ctx_size):
                    size = min(ctx_size, count - part)
                    whole = buffer.at[pl.ds(0, size)]
                    pltpu.make_async_remote_copy(
                        src_ref=whole,
                        dst_ref=whole,
                        send_sem=sem,
                        recv_sem=sem,
                        device_id={"ctx": me},
                        device_id_type=MESH,
                    ).wait_send()

    ring_open(key_all, key_recv, ring_send.at[0], key_length, True)
    cuts = [ctx_size * part // SHARES for part in range(SHARES)] + [ctx_size - 1]
    outgoing = ((1, local_state, state_in), (0, ends_own, ends_all))
    exchange(cuts[0], cuts[1], *outgoing)
    for load in loads[6:]:
        load.wait()

    for g in range(groups):
        turned_q[g] = turn(q_ref[:, g * HEAD_DIM : (g + 1) * HEAD_DIM])

    def score(index):
        return dot(turned_q[...].reshape(groups * TOKENS, LANES), key_all[index], ((1,), (1,)))

    own_score = score(me)
    for g in range(groups):
        masked = jnp.where(causal, own_score[g * TOKENS : (g + 1) * TOKENS], LOWEST)
        score_ref[me, g] = masked
        top_ref[g] = masked

    def key_block(index):
        s = score(index).reshape(groups, TOKENS, LANES)
        score_ref[index] = s
        top_ref[...] = jnp.maximum(top_ref[...], s)

    gram = dot(read_ref[...], write_ref[...], ((1,), (1,)))
    for j in range(pairs):
        x_pair = x_ref[:, j * LANES : (j + 1) * LANES]
        total = None
        for part in range(2):
            h = 2 * j + part
            exponent = jnp.where(causal, cumul[:, h : h + 1] - cumul_t[h : h + 1, :], LOWEST)
            mixing = (jnp.exp(exponent) * gram * step_ref[h : h + 1, :]).astype(BF16)
            keep = first if part == 0 else jnp.logical_not(first)
            term = dot(mixing, jnp.where(keep, x_pair, jnp.zeros_like(x_pair)))
            total = term if total is None else total + term
        skip = jnp.where(
            first[0:1], skip_ref[0:1, 2 * j : 2 * j + 1], skip_ref[0:1, 2 * j + 1 : 2 * j + 2]
        )
        gated_ref[:, j * LANES : (j + 1) * LANES] = total + skip * x_pair.astype(F32)

    total_steps = ring_last(key_length, True)
    done = [0]

    def key_steps(upto):
        upto = min(upto, total_steps)
        if upto > done[0]:
            ring_steps(
                done[0], upto, key_all, key_recv, ring_send.at[0], key_length, True, key_block
            )
        done[0] = max(upto, done[0])

    for part in range(1, SHARES):
        key_steps(STEPS[0][part - 1])
        exchange(cuts[part], cuts[part + 1], *outgoing)
    key_steps(STEPS[0][SHARES - 1])

    exchange_wait(0, ends_all)
    head = lax.div(me * state_rows, MIXER_CHANNELS)
    chosen = jnp.where(row == head, 1.0, 0.0).astype(F32)
    decay_rows[...] = jnp.exp(
        dot(ends_all[...].reshape(ctx_size, LANES), chosen, precision=HIGHEST)
    )
    exchange_wait(1, state_in)

    def scan(b, state):
        state_out[b] = state.astype(BF16)
        return state * decay_rows[pl.ds(b, 1), :] + state_in[b].astype(F32)

    lax.fori_loop(0, ctx_size, scan, jnp.zeros((state_rows, LANES), F32), unroll=8)
    state_back[me] = state_out[me]
    for part in range(SHARES):
        exchange(cuts[part], cuts[part + 1], (2, state_out, state_back))
        key_steps(STEPS[1][part])


    exchange_wait(2, state_back)
    growth = jnp.exp(cumul)
    squares = jnp.zeros((TOKENS, LANES), F32)
    per = LANES // state_rows
    for j in range(pairs):
        at = slice(j * LANES, (j + 1) * LANES)
        state = state_back[j * per : (j + 1) * per].reshape(LANES, LANES)
        inter = dot(read_ref[...], state, ((1,), (1,))) * spread(growth, j)
        gate = gate_ref[:, at].astype(F32)
        gated = (gated_ref[:, at] + inter) * (gate / (1.0 + jnp.exp(-gate)))
        squares = squares + gated * gated
        scaled = gated * gain_ref[0:1, at]
        gated_ref[:, at] = scaled
        scaled_ref[:, at] = scaled.astype(BF16)
    ones = jnp.ones((8, LANES), F32)
    square_own[0] = dot(ones, squares, ((1,), (1,)), precision=HIGHEST)
    square_in[col] = square_own[0]

    def value_terms(e):
        at = pl.ds(pl.multiple_of(e * LANES, LANES), LANES)
        return dot(scaled_ref[...], weight_ref[:, at]).astype(BF16)

    def scatter(i, c):
        order = exp_size // 2 + (1 - 2 * lax.rem(i, 2)) * lax.div(i + 1, 2)
        peer = lax.rem(col + order, exp_size)
        pltpu.make_async_remote_copy(
            src_ref=square_own.at[0],
            dst_ref=square_in.at[col],
            send_sem=exp_send.at[0],
            recv_sem=exp_recv.at[0],
            device_id={"exp": peer},
            device_id_type=MESH,
        ).start()
        terms_ref[peer] = value_terms(peer)
        pltpu.make_async_remote_copy(
            src_ref=terms_ref.at[peer],
            dst_ref=terms_in.at[col],
            send_sem=exp_send.at[1],
            recv_sem=exp_recv.at[1],
            device_id={"exp": peer},
            device_id_type=MESH,
        ).start()
        return c

    lax.fori_loop(0, exp_size - 1, scatter, 0)
    terms_in[col] = value_terms(col)

    key_steps(total_steps)

    for g in range(groups):
        top_ref[g] = jnp.broadcast_to(jnp.max(top_ref[g], axis=1, keepdims=True), (TOKENS, LANES))
        sum_ref[g] = jnp.zeros((TOKENS, LANES), F32)
        out_ref[g] = jnp.zeros((TOKENS, LANES), F32)

    def weigh(b, c):
        for g in range(groups):
            p = jnp.exp2((score_ref[b, g] - top_ref[g]) * EXP2_SCALE)
            sum_ref[g] += p
            prob_ref[b, g] = p.astype(BF16)
        return c

    lax.fori_loop(0, me + 1, weigh, 0)

    def scatter_wait(slot, target, sent=False):
        whole = target.at[pl.ds(0, exp_size - 1)]
        done = pltpu.make_async_remote_copy(
            src_ref=whole,
            dst_ref=whole,
            send_sem=exp_send.at[slot],
            recv_sem=exp_recv.at[slot],
            device_id={"exp": col},
            device_id_type=MESH,
        )
        done.wait_send() if sent else done.wait_recv()

    for slot, target in ((0, square_in), (1, terms_in)):
        scatter_wait(slot, target)
    square_row = square_in[0]
    for e in range(1, exp_size):
        square_row = square_row + square_in[e]
    square = jnp.transpose(jnp.broadcast_to(square_row[0:1, :], (TOKENS, LANES)))
    factor = lax.rsqrt(square * (1.0 / (exp_size * heads * MIXER_CHANNELS)) + NORM_EPS)
    value = terms_in[0].astype(F32)
    for e in range(1, exp_size):
        value = value + terms_in[e].astype(F32)
    value_all[me] = (value * factor).astype(BF16)
    ring_open(value_all, value_recv, ring_send.at[1], value_length, False)

    for j in range(pairs):
        at = slice(j * LANES, (j + 1) * LANES)
        mixer_ref[:, at] = (gated_ref[:, at] * factor).astype(BF16)

    def value_block(index):
        probs = prob_ref[index].reshape(groups * TOKENS, LANES)
        out_ref[...] += dot(probs, value_all[index]).reshape(groups, TOKENS, LANES)

    value_block(me)
    ring_steps(
        0, ring_last(value_length, False), value_all, value_recv, ring_send.at[1], value_length, False, value_block
    )
    for g in range(groups):
        total = jnp.sum(sum_ref[g], axis=1, keepdims=True)
        attn_ref[:, g * HEAD_DIM : (g + 1) * HEAD_DIM] = (out_ref[g] / total).astype(BF16)
    ring_close(key_all, ring_send.at[0], key_length, True)
    ring_close(value_all, ring_send.at[1], value_length, False)
    for slot, target in ((0, ends_all), (1, state_in), (2, state_back)):
        exchange_wait(slot, target, True)
    for slot, target in ((0, square_in), (1, terms_in)):
        scatter_wait(slot, target, True)


def hand_over(attn_in, mixer_in, attn_out, mixer_out, sem):
    first = pltpu.make_async_copy(attn_in, attn_out, sem.at[0])
    second = pltpu.make_async_copy(mixer_in, mixer_out, sem.at[1])
    first.start()
    second.start()
    first.wait()
    second.wait()


SHARES = 2
STEPS = ((2, 4), (6, 8))
SEGMENTS = (1, 2)
PIECES = (1, 1)
INPUTS = 12


def solution(mesh):
    ctx_size, exp_size = mesh.shape["ctx"], mesh.shape["exp"]

    def on_device(
        queries,
        key_rows,
        mixer_input,
        gate_input,
        write_proj,
        read_proj,
        step_size,
        log_decay,
        skip_gain,
        norm_gain,
        value_weight,
    ):
        heads = step_size.shape[1]
        channels = heads * MIXER_CHANNELS
        groups = queries.shape[1] // HEAD_DIM
        state_rows = channels // ctx_size
        frequency = ROPE_BASE ** (-(2.0 * np.arange(HEAD_DIM // 2)) / HEAD_DIM)
        frequency = jnp.asarray(np.tile(frequency, 2)[None, :], F32)
        tile = (TOKENS, LANES)
        anywhere = pl.BlockSpec(memory_space=pl.ANY)
        operands = (
            key_rows,
            log_decay.T,
            step_size.T,
            frequency,
            mixer_input,
            write_proj,
            read_proj,
            queries,
            skip_gain.reshape(1, heads),
            gate_input,
            norm_gain.reshape(1, channels),
            value_weight,
        )
        results = (
            jax.ShapeDtypeStruct(queries.shape, BF16),
            jax.ShapeDtypeStruct(mixer_input.shape, BF16),
        )
        staged = [pltpu.VMEM(a.shape, a.dtype) for a in operands]
        found = pl.pallas_call(
            functools.partial(kernel, ctx_size, exp_size),
            out_shape=tuple(pltpu.VMEM(a.shape, a.dtype) for a in results),
            in_specs=[anywhere] * INPUTS,
            out_specs=(pl.BlockSpec(memory_space=pltpu.VMEM),) * 2,
            scratch_shapes=staged
            + [
                pltpu.SemaphoreType.DMA((INPUTS,)),
                pltpu.VMEM((ctx_size, state_rows, LANES), BF16),
                pltpu.VMEM((ctx_size, state_rows, LANES), BF16),
                pltpu.VMEM((ctx_size, state_rows, LANES), BF16),
                pltpu.VMEM((ctx_size, state_rows, LANES), BF16),
                pltpu.VMEM((1, 1, LANES), F32),
                pltpu.VMEM((ctx_size, 1, LANES), F32),
                pltpu.VMEM(tile, F32),
                pltpu.VMEM(tile, F32),
                pltpu.VMEM((ctx_size, LANES), F32),
                pltpu.VMEM((TOKENS, channels), F32),
                pltpu.VMEM((TOKENS, channels), BF16),
                pltpu.VMEM((exp_size,) + tile, BF16),
                pltpu.VMEM((exp_size,) + tile, BF16),
                pltpu.VMEM((1, 8, LANES), F32),
                pltpu.VMEM((exp_size, 8, LANES), F32),
                pltpu.VMEM((groups,) + tile, BF16),
                pltpu.VMEM((ctx_size,) + tile, BF16),
                pltpu.VMEM((ctx_size,) + tile, BF16),
                pltpu.VMEM((ctx_size, groups) + tile, F32),
                pltpu.VMEM((ctx_size, groups) + tile, BF16),
                pltpu.VMEM((groups,) + tile, F32),
                pltpu.VMEM((groups,) + tile, F32),
                pltpu.VMEM((groups,) + tile, F32),
                pltpu.SemaphoreType.DMA((3,)),
                pltpu.SemaphoreType.DMA((3,)),
                pltpu.SemaphoreType.DMA((2,)),
                pltpu.SemaphoreType.DMA((2,)),
                pltpu.SemaphoreType.DMA((2,)),
                pltpu.SemaphoreType.DMA((ctx_size, PIECES[0])),
                pltpu.SemaphoreType.DMA((ctx_size, PIECES[1])),
            ],
            compiler_params=pltpu.CompilerParams(
                collective_id=0, has_side_effects=True, vmem_limit_bytes=56 * 1024 * 1024
            ),
        )(*operands)
        return pl.pallas_call(
            hand_over,
            out_shape=results,
            in_specs=[pl.BlockSpec(memory_space=pltpu.VMEM)] * 2,
            out_specs=(anywhere, anywhere),
            scratch_shapes=[pltpu.SemaphoreType.DMA((2,))],
            compiler_params=pltpu.CompilerParams(vmem_limit_bytes=2 * 1024 * 1024),
        )(*found)

    return jax.shard_map(
        on_device,
        mesh=mesh,
        in_specs=(
            P("ctx", "exp"),
            P("ctx", "exp"),
            P("ctx", "exp"),
            P("ctx", "exp"),
            P("ctx", None),
            P("ctx", None),
            P("ctx", "exp"),
            P("ctx", "exp"),
            P("exp"),
            P("exp"),
            P("exp", None),
        ),
        out_specs=(P("ctx", "exp"), P("ctx", "exp")),
        check_vma=False,
    )
```
